32 devices in a mesh: row: 4 (over y, x), col: 8 (over z, core).
Axes of the slice: x: 2, y: 2, z: 4, core: 2. Of those that a mesh axis runs over, the one named last changes fastest.
Arguments:
- weights: bfloat16 [3072, 3072], P('col', 'row'), may hold values from -0.109375 to 0.109375
- weight_flags: int32 [24, 24], P('col', 'row'), may hold values from 0 to 1, as said below
- hamiltonian: bfloat16 [3072, 4096], P('row', 'col'), may hold values from -6 to 6
- ham_flags: int32 [24, 32], P('row', 'col'), may hold values from 0 to 1, as said below
Outputs:
- coupling: bfloat16 [3072, 4096], P('row', 'col')
The draws below stay inside these ranges and needn't reach their ends.
Inputs may be any that keep to these rules, and one draw needn't show every extreme that they name: `weight_flags`: 1 marks a stored block of W, 0 an absent one; the share of stored blocks differs from block row to block row. `ham_flags`: 1 marks a stored block of the slab, 0 an absent one; the share of stored blocks differs from block row to block row.
All inputs are finite; a program needn't handle non-finite values.
Results may differ from the reference program's by a relative error of at most 0.001.
Values may be sent and summed in bfloat16 or wider, within the bound.
A program may use at most 64 MiB of HBM per device.

```python
import jax
import jax.numpy as jnp
from jax import lax

BLOCK = 128
RB = 6
SC = 4
STEPS = 4
MB = 24
SB = 32
N = 3072
S = 4096
N_ROW = 4
N_COL = 8


def draw_weight_flags(key, part):
    row_ids = jnp.arange(MB, dtype=jnp.int32)[:, None]
    threshold = 30 + 65 * (row_ids * 7 % MB) // MB
    rolled = jax.random.randint(key, (MB, MB), 0, 100)
    return (rolled < threshold).astype(jnp.int32)


def draw_ham_flags(key, part):
    row_ids = jnp.arange(MB, dtype=jnp.int32)[:, None]
    threshold = 35 + 60 * ((row_ids * 5 + 3) % MB) // MB
    rolled = jax.random.randint(jax.random.fold_in(key, 11), (MB, SB), 0, 100)
    return (rolled < threshold).astype(jnp.int32)


def steps_of(stream_key, dims, cuts, least, high):
    def one(position, parts):
        steps = jax.random.uniform(jax.random.fold_in(jax.random.fold_in(stream_key, 6), position), (parts,), jnp.float32, least / len(cuts), high / len(cuts))
        return jnp.repeat(jnp.exp(steps), dims[position] // parts).reshape((-1,) + (1,) * (len(dims) - position - 1))

    loudness = one(*cuts[0])
    for cut in cuts[1:]:
        loudness = loudness * one(*cut)
    return loudness


def normal_values(stream_key, shape, scale, bound, shards=(), kind=jnp.bfloat16):
    loudness = steps_of(stream_key, shape, shards, -0.22, 0.18) if shards else 1.0
    entries = jax.random.normal(stream_key, shape, jnp.float32) * scale * loudness
    return jnp.minimum(jnp.maximum(entries, -bound), bound).astype(kind)


def setup_inputs(seed: int = 0) -> dict:
    streams_of = jax.random.split(jax.random.key(seed), 5)
    return {
        "weights": normal_values(streams_of[0], (N, N), (STEPS * RB * BLOCK) ** -0.5, 0.109375, ((0, 8), (1, 4))),
        "weight_flags": draw_weight_flags(jax.random.fold_in(streams_of[4], 71), 0),
        "hamiltonian": normal_values(streams_of[2], (N, S), 1.0, 6.0, ((0, 4), (1, 8))),
        "ham_flags": draw_ham_flags(jax.random.fold_in(streams_of[4], 71), 0),
    }


def masked(dense_tile, flag_grid):
    row_blocks, col_blocks = flag_grid.shape
    block_edge = dense_tile.shape[0] // row_blocks
    shaped = dense_tile.reshape(row_blocks, block_edge, col_blocks, block_edge)
    retain = (flag_grid > 0)[:, None, :, None]
    return jnp.where(retain, shaped, jnp.zeros_like(shaped)).reshape(dense_tile.shape)


def reference(weights, weight_flags, hamiltonian, ham_flags):
    w_masked = masked(weights, weight_flags)
    h_masked = masked(hamiltonian, ham_flags)
    panel_rows = RB * BLOCK
    pair_count = N_COL // 2
    w_panels = w_masked.reshape(N_ROW, panel_rows, N_ROW, panel_rows)
    h_panels = h_masked.reshape(N_ROW, panel_rows, pair_count, 2 * SC * BLOCK)
    pair_ids = jnp.arange(pair_count, dtype=jnp.int32)

    def one_piece(piece_index):
        w_piece = lax.dynamic_index_in_dim(w_panels, piece_index, 2, keepdims=False)
        summed = jnp.zeros((pair_count, panel_rows, 2 * SC * BLOCK), jnp.float32)
        for step_index in range(STEPS):
            chosen = ((piece_index + pair_ids + step_index) % N_ROW).astype(jnp.int32)
            w_chosen = w_piece[chosen].astype(jnp.float32)
            h_chosen = h_panels[chosen, :, pair_ids, :].astype(jnp.float32)
            summed = summed + jnp.einsum("pkm,pkn->pmn", w_chosen, h_chosen, precision=lax.Precision.HIGHEST)
        return jnp.transpose(summed, (1, 0, 2)).reshape(panel_rows, pair_count * 2 * SC * BLOCK)

    pieces = lax.map(one_piece, jnp.arange(N_ROW, dtype=jnp.int32))
    return pieces.reshape(N, S).astype(jnp.bfloat16)
```

```python
import functools

import jax
import jax.numpy as jnp
from jax import lax
from jax.experimental import pallas as pl
from jax.experimental.pallas import tpu as pltpu
from jax.sharding import PartitionSpec as P

STEPS = 4


def from_behind(block, axis, distance):
    devices = range(lax.axis_size(axis))
    route = [((i - distance) % len(devices), i) for i in devices]
    return lax.ppermute(block, axis, route)


def from_partner(value, axis, bit):
    mask = 2**bit
    pairs = [(source, source ^ mask) for source in range(lax.axis_size(axis))]
    return lax.ppermute(value, axis, pairs)


def masked(dense_tile, flag_grid):
    row_blocks, col_blocks = flag_grid.shape
    block_edge = dense_tile.shape[0] // row_blocks
    shaped = dense_tile.reshape(row_blocks, block_edge, col_blocks, block_edge)
    retain = (flag_grid > 0)[:, None, :, None]
    return jnp.where(retain, shaped, jnp.zeros_like(shaped)).reshape(dense_tile.shape)


def aligned(operand, amount, bit_count, mover):
    for level in range(bit_count):
        moved = mover(operand, level)
        chosen = (amount >> level) % 2 == 1
        operand = jnp.where(chosen, moved, operand)
    return operand


def contract(left_part, right_part):
    return lax.dot_general(
        left_part, right_part, (((0,), (0,)), ((), ())), preferred_element_type=jnp.float32
    )


def shards(weights, weight_flags, hamiltonian, ham_flags):
    row_count = lax.axis_size("row")
    bit_count = (row_count - 1).bit_length()
    row_index = lax.axis_index("row")
    col_index = lax.axis_index("col")
    pair_index = col_index // 2
    parity = col_index % 2
    w_masked = masked(weights, weight_flags)
    h_masked = masked(hamiltonian, ham_flags)
    ham_tile = aligned(
        h_masked,
        pair_index,
        bit_count,
        lambda operand, level: from_behind(operand, "row", -(1 << level)),
    )
    w_half = aligned(
        w_masked,
        row_index,
        bit_count,
        lambda operand, level: from_behind(operand, "col", -(2 << level)),
    )
    half_rows = ham_tile.shape[0] // 2
    upper_rows = ham_tile[:half_rows]
    lower_rows = ham_tile[half_rows:]
    retained = jnp.where(parity == 0, upper_rows, lower_rows)
    handed = jnp.where(parity == 0, lower_rows, upper_rows)
    received = from_partner(handed, "col", 0)
    joined = jnp.where(
        parity == 0,
        jnp.concatenate((retained, received), 1),
        jnp.concatenate((received, retained), 1),
    )
    summed = contract(w_half, joined)
    for step_index in range(1, STEPS):
        w_half = from_behind(w_half, "col", -2)
        joined = from_behind(joined, "row", -1)
        summed = summed + contract(w_half, joined)
    half_width = summed.shape[1] // 2
    own_part = jnp.where(parity == 0, summed[:, :half_width], summed[:, half_width:])
    their_part = jnp.where(parity == 0, summed[:, half_width:], summed[:, :half_width])
    summed = own_part + from_partner(their_part, "col", 0)
    return summed.astype(jnp.bfloat16)


SHARES = (5, 3)
CHUNKS = len(SHARES)
MESH = pl.DeviceIdType.MESH


def put(source, target, sent, landed, device):
    return pltpu.make_async_remote_copy(
        src_ref=source,
        dst_ref=target,
        send_sem=sent,
        recv_sem=landed,
        device_id=device,
        device_id_type=MESH,
    )


def gather_kernel(
    panels, w_flags_hbm, h_flags_hbm, w_hbm, h_hbm, out_ref, w_flags, h_flags, w_ref, h_ref, w_buf, h_buf, total,
    loaded, w_landed, up_sent, down_sent, core_sent, h_landed, h_sent,
):
    row = lax.axis_index("row")
    col = lax.axis_index("col")
    pair = col // 2
    core = col % 2
    partner = (row, pair * 2 + 1 - core)
    above = (row, col + 2)
    below = (row, col - 2)
    beside = row + 1 - 2 * (row % 2)
    across = (row + panels // 2) % panels
    opposite = (beside + panels // 2) % panels
    has_above = pair < panels - 1
    has_below = pair > 0

    loads = [
        pltpu.make_async_copy(source, target, loaded.at[n])
        for n, (source, target) in enumerate(
            ((w_flags_hbm, w_flags), (w_hbm, w_ref), (h_flags_hbm, h_flags), (h_hbm, h_ref))
        )
    ]
    for load in loads:
        load.start()

    barrier = pltpu.get_barrier_semaphore()

    def greet(device):
        pl.semaphore_signal(barrier, inc=1, device_id=device, device_id_type=MESH)

    greet(partner)
    greet((beside, col))
    greet((across, col))

    @pl.when(has_above)
    def _():
        greet(above)

    @pl.when(has_below)
    def _():
        greet(below)

    loads[0].wait()
    loads[1].wait()
    half_rows, width = w_ref.shape
    edge = half_rows // w_flags.shape[0]
    bounds = [half_rows * sum(SHARES[:k]) // sum(SHARES) for k in range(CHUNKS + 1)]
    for r in range(w_flags.shape[0]):
        for c in range(w_flags.shape[1]):
            rows, lanes = slice(r * edge, (r + 1) * edge), slice(c * edge, (c + 1) * edge)
            block = w_ref[rows, lanes]
            kept = jnp.where(w_flags[r, c] > 0, block, jnp.zeros_like(block))
            w_buf[pair, core, rows, lanes] = kept
    pl.semaphore_wait(
        barrier, 3 + has_above.astype(jnp.int32) + has_below.astype(jnp.int32)
    )

    def piece(k):
        return slice(bounds[k], bounds[k + 1])

    def go_up(panel, k):
        slot = w_buf.at[panel, core, piece(k)]
        return put(slot, slot, up_sent.at[panel, k], w_landed.at[panel, core, k], above)

    def go_down(panel, k):
        slot = w_buf.at[panel, core, piece(k)]
        return put(slot, slot, down_sent.at[panel, k], w_landed.at[panel, core, k], below)

    def go_over(panel, k):
        slot = w_buf.at[panel, core, piece(k)]
        return put(slot, slot, core_sent.at[panel, k], w_landed.at[panel, core, k], partner)

    def arrival(panel, half, k):
        slot = w_buf.at[panel, half, piece(k)]
        return put(slot, slot, core_sent.at[panel, k], w_landed.at[panel, half, k], partner)

    def h_put(panel, half, number, device):
        slot = h_buf.at[panel, half]
        return put(slot, slot, h_sent.at[number], h_landed.at[panel, half], device)

    def each(body):
        for k in range(CHUNKS):
            body(k)

    def first_sends(k):
        @pl.when(has_above)
        def _():
            go_up(pair, k).start()

        @pl.when(has_below)
        def _():
            go_down(pair, k).start()

    each(first_sends)
    loads[2].wait()
    loads[3].wait()
    for r in range(h_flags.shape[1]):
        for c in range(h_flags.shape[0]):
            lanes = slice(c * edge, (c + 1) * edge)
            block = h_ref[r * edge:(r + 1) * edge, lanes]
            half, start = divmod(r * edge, half_rows)
            kept = jnp.where(h_flags[c, r] > 0, block, jnp.zeros_like(block))
            h_buf[row, half, start:start + edge, lanes] = kept

    h_copies = [
        h_put(row, 0, 0, (beside, col)),
        h_put(row, 1, 1, (across, col)),
        h_put(row, 1, 2, (beside, col)),
        h_put(row, 0, 3, (across, col)),
    ]
    for copy in h_copies:
        copy.start()
    each(lambda k: go_over(pair, k).start())

    def relay(distance, k):
        @pl.when(pair >= distance)
        def _():
            panel = pair - distance
            arrival(panel, core, k).wait_recv()

            @pl.when(has_above)
            def _():
                go_up(panel, k).start()

            go_over(panel, k).start()

        @pl.when(pair + distance < panels)
        def _():
            panel = pair + distance
            arrival(panel, core, k).wait_recv()

            @pl.when(has_below)
            def _():
                go_down(panel, k).start()

            go_over(panel, k).start()

    each(functools.partial(relay, 1))
    h_put(beside, 0, 0, (beside, col)).wait_recv()
    relay_across = h_put(beside, 0, 4, (across, col))
    relay_across.start()
    h_put(across, 1, 0, (beside, col)).wait_recv()
    relay_beside = h_put(across, 1, 5, (beside, col))
    relay_beside.start()
    for distance in range(2, panels - 1):
        each(functools.partial(relay, distance))
    h_put(beside, 1, 0, (beside, col)).wait_recv()
    h_put(across, 0, 0, (beside, col)).wait_recv()
    h_put(opposite, 0, 0, (beside, col)).wait_recv()
    h_put(opposite, 1, 0, (beside, col)).wait_recv()

    total[...] = jnp.zeros_like(total)
    span = 2 * half_rows

    def near_panel(step, carry):
        panel = (pair + step) % panels
        gap = panel - pair

        @pl.when((gap < panels - 1) & (gap > 1 - panels))
        def _():
            each(lambda k: arrival(panel, 1 - core, k).wait_recv())
            left = w_buf[panel].reshape(span, width)
            right = h_buf[panel].reshape(span, h_buf.shape[3])
            total[...] += contract(left, right)

        return carry

    lax.fori_loop(0, panels, near_panel, 0)

    is_end = (pair == 0) | (pair == panels - 1)

    @pl.when(is_end)
    def _():
        panel = panels - 1 - pair

        def product(half, k):
            return contract(w_buf[panel, half, piece(k)], h_buf[panel, half, piece(k)])

        for k in range(CHUNKS - 1):
            arrival(panel, core, k).wait_recv()
            go_over(panel, k).start()
            total[...] += product(core, k)
            arrival(panel, 1 - core, k).wait_recv()
            total[...] += product(1 - core, k)

        last = CHUNKS - 1
        arrival(panel, core, last).wait_recv()
        go_over(panel, last).start()
        total[...] += product(core, last)
        arrival(panel, 1 - core, last).wait_recv()
        out_ref[...] = (total[...] + product(1 - core, last)).astype(out_ref.dtype)

    @pl.when(jnp.logical_not(is_end))
    def _():
        out_ref[...] = total[...].astype(out_ref.dtype)

    for copy in h_copies + [relay_across, relay_beside]:
        copy.wait_send()

    def drain(panel, carry):
        def one(k):
            go_over(panel, k).wait_send()

            @pl.when(has_above & (panel <= pair))
            def _():
                go_up(panel, k).wait_send()

            @pl.when(has_below & (panel >= pair))
            def _():
                go_down(panel, k).wait_send()

        each(one)
        return carry

    lax.fori_loop(0, panels, drain, 0)


def gathered(weights, weight_flags, hamiltonian, ham_flags):
    panels = lax.axis_size("row")
    half_rows, width = weights.shape
    panel_rows, slice_cols = hamiltonian.shape
    dma = pltpu.SemaphoreType.DMA
    vmem = pl.BlockSpec(memory_space=pltpu.VMEM)
    hbm = pl.BlockSpec(memory_space=pl.ANY)
    return pl.pallas_call(
        functools.partial(gather_kernel, panels),
        out_shape=pltpu.VMEM((width, slice_cols), jnp.bfloat16),
        in_specs=[hbm] * 4,
        out_specs=vmem,
        scratch_shapes=[
            pltpu.SMEM(weight_flags.shape, weight_flags.dtype),
            pltpu.SMEM(ham_flags.shape[::-1], ham_flags.dtype),
            pltpu.VMEM(weights.shape, weights.dtype),
            pltpu.VMEM(hamiltonian.shape, hamiltonian.dtype),
            pltpu.VMEM((panels, 2, half_rows, width), jnp.bfloat16),
            pltpu.VMEM((panels, 2, panel_rows // 2, slice_cols), jnp.bfloat16),
            pltpu.VMEM((width, slice_cols), jnp.float32),
            dma((4,)),
            dma((panels, 2, CHUNKS)),
            dma((panels, CHUNKS)),
            dma((panels, CHUNKS)),
            dma((panels, CHUNKS)),
            dma((panels, 2)),
            dma((6,)),
        ],
        compiler_params=pltpu.CompilerParams(collective_id=0, has_side_effects=True),
    )(weight_flags, ham_flags.T, weights, hamiltonian)


def packed_kernel(
    panels, w_flags_hbm, h_flags_hbm, w_hbm, h_hbm, out_ref, over_ref,
    h_flags, same_flags, other_flags, first_from, spill, starts, totals, line_over,
    w_blocks, h_ref, same, other, from_above, from_below, to_below, to_above, w_buf, h_buf, total,
    loaded, same_landed, other_landed, down_sent, up_sent, core_sent,
    shared_landed, shared_sent, shared_core_sent, h_landed, h_sent, over_landed, over_sent,
):
    row = lax.axis_index("row")
    col = lax.axis_index("col")
    pair = col // 2
    core = col % 2
    partner = (row, pair * 2 + 1 - core)
    above = (row, col + 2)
    below = (row, col - 2)
    beside = row + 1 - 2 * (row % 2)
    across = (row + panels // 2) % panels
    opposite = (beside + panels // 2) % panels
    top = panels - 1
    has_above = pair < top
    has_below = pair > 0
    home = top
    w_flags = same_flags[home]
    row_blocks, col_blocks = w_flags.shape
    blocks, edge = w_blocks.shape[0], w_blocks.shape[1]
    half_rows = row_blocks * edge
    shared = from_above.shape[0]
    part = shared // 2
    base = base_slots(blocks)
    early = early_slots(blocks)
    rest = blocks - base
    slices = (slice(0, early), slice(early, base))
    FLAGS, WHOLE = 2, 0

    flag_load = pltpu.make_async_copy(w_flags_hbm, w_flags, loaded.at[0])
    flag_load.start()
    w_loads = []
    for b in range(blocks):
        r, c = divmod(b, col_blocks)
        source = w_hbm.at[r * edge:(r + 1) * edge, c * edge:(c + 1) * edge]
        load = pltpu.make_async_copy(source, w_blocks.at[b], loaded.at[3 + b])
        load.start()
        w_loads.append(load)
    h_loads = [
        pltpu.make_async_copy(h_flags_hbm, h_flags, loaded.at[1]),
        pltpu.make_async_copy(h_hbm, h_ref, loaded.at[2]),
    ]
    for load in h_loads:
        load.start()

    barrier = pltpu.get_barrier_semaphore()

    def greet(device):
        pl.semaphore_signal(barrier, inc=1, device_id=device, device_id_type=MESH)

    greet(partner)
    greet((beside, col))
    greet((across, col))

    @pl.when(has_above)
    def _():
        greet(above)

    @pl.when(has_below)
    def _():
        greet(below)

    def piece(refs, flags, o, k):
        return flags[o] if k == FLAGS else refs[o].at[slices[k]]

    def go_down(d, k):
        source, target = (piece(same, same_flags, home + n, k) for n in (d, d + 1))
        return put(source, target, down_sent.at[d, k], same_landed.at[home + d + 1, k], below)

    def go_up(d, k):
        source, target = (piece(same, same_flags, home - n, k) for n in (d, d + 1))
        return put(source, target, up_sent.at[d, k], same_landed.at[home - d - 1, k], above)

    def go_over(o, k):
        if o == home and k == WHOLE:
            source, target = same[o], other[o]
        else:
            source, target = piece(same, same_flags, o, k), piece(other, other_flags, o, k)
        return put(source, target, core_sent.at[o, k], other_landed.at[o, k], partner)

    def landed(o, k):
        slot = piece(same, same_flags, o, k)
        return put(slot, slot, core_sent.at[o, k], same_landed.at[o, k], partner)

    def crossed(o, k):
        return go_over(o, k)

    def shared_half(ref, half):
        return ref.at[pl.ds(half * part, part)]

    def shared_down():
        return put(to_below, shared_half(from_above, core), shared_sent.at[0], shared_landed.at[0, 0], below)

    def shared_up():
        return put(to_above, shared_half(from_below, core), shared_sent.at[1], shared_landed.at[1, 0], above)

    def shared_over(side):
        slot = shared_half((from_above, from_below)[side], core)
        return put(slot, slot, shared_core_sent.at[side], shared_landed.at[side, 1], partner)

    def shared_arrival(side):
        slot = shared_half((from_above, from_below)[side], core)
        return put(slot, slot, shared_core_sent.at[side], shared_landed.at[side, 0], partner)

    def shared_crossed(side):
        slot = shared_half((from_above, from_below)[side], 1 - core)
        return put(slot, slot, shared_core_sent.at[side], shared_landed.at[side, 1], partner)

    def h_put(panel, half, number, device):
        slot = h_buf.at[panel, half]
        return put(slot, slot, h_sent.at[number], h_landed.at[panel, half], device)

    flag_load.wait()
    nearest = jnp.int32(blocks - 1)
    first_from[blocks] = nearest
    for b in reversed(range(blocks)):
        nearest = jnp.where(w_flags[divmod(b, col_blocks)] > 0, b, nearest)
        first_from[b] = nearest
    for load in w_loads:
        load.wait()

    def pack(start, stop, chosen):
        for k in range(start, stop):
            same[home][k] = w_blocks[chosen]
            chosen = first_from[chosen + 1]
        return chosen

    chosen = pack(0, early, first_from[0])
    pl.semaphore_wait(
        barrier, 3 + has_above.astype(jnp.int32) + has_below.astype(jnp.int32)
    )

    def both_ways(k, down, up):
        @pl.when(down)
        def _():
            go_down(0, k).start()

        @pl.when(up)
        def _():
            go_up(0, k).start()

    both_ways(0, has_below, has_above)
    both_ways(FLAGS, has_below, has_above)
    go_over(home, FLAGS).start()
    chosen = pack(early, base, chosen)
    both_ways(1, has_below & (pair < top), has_above & (pair > 0))
    pack(base, blocks, chosen)
    go_over(home, WHOLE).start()

    for load in h_loads:
        load.wait()
    for r in range(h_flags.shape[1]):
        for c in range(h_flags.shape[0]):
            lanes = slice(c * edge, (c + 1) * edge)
            block = h_ref[r * edge:(r + 1) * edge, lanes]
            half, start = divmod(r * edge, half_rows)
            kept = jnp.where(h_flags[c, r] > 0, block, jnp.zeros_like(block))
            h_buf[row, half, start:start + edge, lanes] = kept

    h_copies = [
        h_put(row, 0, 0, (beside, col)),
        h_put(row, 1, 1, (across, col)),
        h_put(row, 1, 2, (beside, col)),
        h_put(row, 0, 3, (across, col)),
    ]
    for copy in h_copies:
        copy.start()

    def beyond(flags):
        count = jnp.int32(0)
        for r in range(row_blocks):
            for c in range(col_blocks):
                count = count + (flags[r, c] > 0).astype(jnp.int32)
        return jnp.maximum(count - base, 0)

    crossed(home, FLAGS).wait_recv()
    own_same = beyond(w_flags)
    own_other = beyond(other_flags[home])
    own_both = own_same + own_other
    same_start = jnp.where(core == 0, 0, own_other)
    other_start = jnp.where(core == 0, own_same, 0)

    def within(index, limit):
        return jnp.minimum(jnp.maximum(index, 0), limit - 1)

    def share(target, source):
        for n in range(part):
            slot = core * part + n
            in_same, in_other = slot - same_start, slot - other_start
            value = other[home][base + within(in_other, rest)]
            if source is not None:
                passed = source[within(slot - own_both, shared)]
                value = jnp.where((in_other >= 0) & (in_other < own_other), value, passed)
            mine = same[home][base + within(in_same, rest)]
            target[n] = jnp.where((in_same >= 0) & (in_same < own_same), mine, value)

    crossed(home, WHOLE).wait_recv()

    @pl.when(pair == top)
    def _():
        share(to_below, None)
        shared_down().start()
        go_down(0, 1).start()

    @pl.when(pair == 0)
    def _():
        share(to_above, None)
        shared_up().start()
        go_up(0, 1).start()

    def dense(flags, packed, panel, half):
        position = jnp.int32(0)
        for r in range(row_blocks):
            for c in range(col_blocks):
                block = packed[position]
                present = flags[r, c] > 0
                rows, lanes = slice(r * edge, (r + 1) * edge), slice(c * edge, (c + 1) * edge)
                w_buf[panel, half, rows, lanes] = jnp.where(present, block, jnp.zeros_like(block))
                position = position + present.astype(jnp.int32)

    dense(w_flags, same[home], pair, core)
    dense(other_flags[home], other[home], pair, 1 - core)
    total[...] = jnp.zeros_like(total)

    def forward(d, k):
        @pl.when(pair + d <= top)
        def _():
            landed(home + d, k).wait_recv()

            @pl.when(has_below)
            def _():
                go_down(d, k).start()

            go_over(home + d, k).start()

        @pl.when(pair - d >= 0)
        def _():
            landed(home - d, k).wait_recv()

            @pl.when(has_above)
            def _():
                go_up(d, k).start()

            go_over(home - d, k).start()

    def receive(d, k):
        @pl.when(pair + d <= top)
        def _():
            landed(home + d, k).wait_recv()
            go_over(home + d, k).start()

        @pl.when(pair - d >= 0)
        def _():
            landed(home - d, k).wait_recv()
            go_over(home - d, k).start()

    def middle(d):
        @pl.when(pair + d < top)
        def _():
            landed(home + d, 1).wait_recv()

            @pl.when(has_below)
            def _():
                go_down(d, 1).start()

            go_over(home + d, 1).start()

        @pl.when(pair - d > 0)
        def _():
            landed(home - d, 1).wait_recv()

            @pl.when(has_above)
            def _():
                go_up(d, 1).start()

            go_over(home - d, 1).start()

    def last(d):
        @pl.when(pair + d == top)
        def _():
            shared_arrival(0).wait_recv()
            shared_over(0).start()
            shared_crossed(0).wait_recv()

            @pl.when(has_below)
            def _():
                share(to_below, from_above)
                shared_down().start()

            landed(home + d, 1).wait_recv()

            @pl.when(has_below)
            def _():
                go_down(d, 1).start()

            go_over(home + d, 1).start()

        @pl.when(pair - d == 0)
        def _():
            shared_arrival(1).wait_recv()
            shared_over(1).start()
            shared_crossed(1).wait_recv()

            @pl.when(has_above)
            def _():
                share(to_above, from_below)
                shared_up().start()

            landed(home - d, 1).wait_recv()

            @pl.when(has_above)
            def _():
                go_up(d, 1).start()

            go_over(home - d, 1).start()

    forward(1, FLAGS)
    forward(1, 0)
    h_put(beside, 0, 0, (beside, col)).wait_recv()
    relay_across = h_put(beside, 0, 4, (across, col))
    relay_across.start()
    h_put(across, 1, 0, (beside, col)).wait_recv()
    relay_beside = h_put(across, 1, 5, (beside, col))
    relay_beside.start()
    middle(1)
    forward(2, FLAGS)
    last(1)
    forward(2, 0)
    receive(3, FLAGS)
    middle(2)

    totals[0] = jnp.where(pair > 0, own_both, 0)
    totals[1] = jnp.where(pair < top, own_both, 0)
    for side, way in ((0, 1), (1, -1)):
        starts[home, side] = jnp.int32(0)
        for d in range(1, panels):
            o, n = home + way * d, pair + way * d

            @pl.when((n >= 0) & (n <= top))
            def _(o=o, n=n, side=side):
                crossed(o, FLAGS).wait_recv()
                at_same, at_other = beyond(same_flags[o]), beyond(other_flags[o])
                start = starts[home, side]
                starts[o, 0] = start + jnp.where(core == 0, 0, at_other)
                starts[o, 1] = start + jnp.where(core == 0, at_same, 0)
                starts[home, side] = start + at_same + at_other
                totals[0] += jnp.where(n > 0, at_same + at_other, 0)
                totals[1] += jnp.where(n < top, at_same + at_other, 0)

    line_over[0, 0] = jnp.maximum(totals[0] - shared, 0) + jnp.maximum(totals[1] - shared, 0)

    def agree(n, device):
        return put(line_over.at[2 * n], line_over.at[2 * n + 1], over_sent.at[n], over_landed.at[n], device)

    agree(0, (beside, col)).start()
    last(2)
    agree(0, (beside, col)).wait_recv()
    line_over[2, 0] = line_over[0, 0] + line_over[1, 0]
    agree(1, (across, col)).start()

    def fill(o, side):
        source = (from_above, from_below)[side]
        for n in range(rest):
            same[o][base + n] = source[within(starts[o, 0] + n, shared)]
            other[o][base + n] = source[within(starts[o, 1] + n, shared)]

    def spread(o, way_d):
        dense(same_flags[o], same[o], pair + way_d, core)
        dense(other_flags[o], other[o], pair + way_d, 1 - core)

    h_put(beside, 1, 0, (beside, col)).wait_recv()
    h_put(across, 0, 0, (beside, col)).wait_recv()
    far = top

    @pl.when(pair + far == top)
    def _():
        landed(home + far, 0).wait_recv()
        go_over(home + far, 0).start()
        shared_arrival(0).wait_recv()
        shared_over(0).start()

    @pl.when(pair - far == 0)
    def _():
        landed(home - far, 0).wait_recv()
        go_over(home - far, 0).start()
        shared_arrival(1).wait_recv()
        shared_over(1).start()

    h_put(opposite, 0, 0, (beside, col)).wait_recv()
    h_put(opposite, 1, 0, (beside, col)).wait_recv()
    span = 2 * half_rows
    width = col_blocks * edge

    def add(panel):
        left = w_buf[panel].reshape(span, width)
        right = h_buf[panel].reshape(span, h_buf.shape[3])
        total[...] += contract(left, right)

    def one_panel(step, carry):
        add((pair + step) % panels)
        return carry

    add(pair)

    @pl.when(pair + far == top)
    def _():
        shared_crossed(0).wait_recv()

    @pl.when(pair - far == 0)
    def _():
        shared_crossed(1).wait_recv()

    for side, way in ((0, 1), (1, -1)):
        for d in range(1, far):
            o, n = home + way * d, pair + way * d

            @pl.when((n >= 0) & (n <= top))
            def _(o=o, side=side, way=way, d=d):
                for k in range(2):
                    crossed(o, k).wait_recv()
                fill(o, side)
                spread(o, way * d)

    def near_panel(step, carry):
        panel = (pair + step) % panels
        gap = panel - pair

        @pl.when((gap < far) & (gap > -far))
        def _():
            add(panel)

        return carry

    lax.fori_loop(1, panels, near_panel, 0)

    is_end = (pair == 0) | (pair == top)
    for side, way in ((0, 1), (1, -1)):
        o = home + way * far

        @pl.when(pair == (0, top)[side])
        def _(o=o, side=side, way=way):
            landed(o, 1).wait_recv()
            go_over(o, 1).start()
            crossed(o, 0).wait_recv()
            fill(o, side)
            dense(same_flags[o], same[o], pair + way * far, core)

    @pl.when(is_end)
    def _():
        panel = top - pair
        total[...] += contract(w_buf[panel, core], h_buf[panel, core])

    for side, way in ((0, 1), (1, -1)):
        o = home + way * far

        @pl.when(pair == (0, top)[side])
        def _(o=o, side=side, way=way):
            crossed(o, 1).wait_recv()
            dense(other_flags[o], other[o], pair + way * far, 1 - core)

    @pl.when(is_end)
    def _():
        panel = top - pair
        final = total[...] + contract(w_buf[panel, 1 - core], h_buf[panel, 1 - core])
        out_ref[...] = final.astype(out_ref.dtype)

    @pl.when(jnp.logical_not(is_end))
    def _():
        out_ref[...] = total[...].astype(out_ref.dtype)

    agree(1, (across, col)).wait_recv()
    over_ref[0, 0] = line_over[2, 0] + line_over[3, 0]
    for n in range(2):
        agree(n, (beside, col)).wait_send()
    for copy in h_copies + [relay_across, relay_beside]:
        copy.wait_send()
    go_over(home, FLAGS).wait_send()
    go_over(home, WHOLE).wait_send()

    @pl.when(has_above)
    def _():
        shared_over(0).wait_send()
        shared_up().wait_send()

    @pl.when(has_below)
    def _():
        shared_over(1).wait_send()
        shared_down().wait_send()

    for d in range(far):
        @pl.when(has_below & (pair + d <= top))
        def _(d=d):
            for k in range(3):
                go_down(d, k).wait_send()

        @pl.when(has_above & (pair - d >= 0))
        def _(d=d):
            for k in range(3):
                go_up(d, k).wait_send()

    for d in range(1, panels):
        @pl.when(pair + d <= top)
        def _(d=d):
            for k in range(3):
                go_over(home + d, k).wait_send()

        @pl.when(pair - d >= 0)
        def _(d=d):
            for k in range(3):
                go_over(home - d, k).wait_send()


def base_slots(blocks):
    return 2 * blocks // 3


def early_slots(blocks):
    return 2 * base_slots(blocks) // 3


def packed(weights, weight_flags, hamiltonian, ham_flags):
    panels = lax.axis_size("row")
    half_rows, width = weights.shape
    panel_rows, slice_cols = hamiltonian.shape
    edge = half_rows // weight_flags.shape[0]
    blocks = weight_flags.size
    shared = base_slots(blocks)
    offsets = 2 * panels - 1
    dma = pltpu.SemaphoreType.DMA
    hbm = pl.BlockSpec(memory_space=pl.ANY)

    def many(shape, dtype, space):
        return [space(shape, dtype) for _ in range(offsets)]

    def slots(count):
        return pltpu.VMEM((count, edge, edge), jnp.bfloat16)

    out, over = pl.pallas_call(
        functools.partial(packed_kernel, panels),
        out_shape=(
            pltpu.VMEM((width, slice_cols), jnp.bfloat16),
            jax.ShapeDtypeStruct((1, 1), jnp.int32),
        ),
        in_specs=[hbm] * 4,
        out_specs=(pl.BlockSpec(memory_space=pltpu.VMEM), pl.BlockSpec(memory_space=pltpu.SMEM)),
        scratch_shapes=[
            pltpu.SMEM(ham_flags.shape[::-1], ham_flags.dtype),
            many(weight_flags.shape, weight_flags.dtype, pltpu.SMEM),
            many(weight_flags.shape, weight_flags.dtype, pltpu.SMEM),
            pltpu.SMEM((blocks + 1,), jnp.int32),
            pltpu.SMEM((offsets, 2), jnp.int32),
            pltpu.SMEM((offsets, 2), jnp.int32),
            pltpu.SMEM((2,), jnp.int32),
            pltpu.SMEM((4, 1), jnp.int32),
            slots(blocks),
            pltpu.VMEM(hamiltonian.shape, hamiltonian.dtype),
            [slots(blocks) for _ in range(offsets)],
            [slots(blocks) for _ in range(offsets)],
            slots(shared),
            slots(shared),
            slots(shared // 2),
            slots(shared // 2),
            pltpu.VMEM((panels, 2, half_rows, width), jnp.bfloat16),
            pltpu.VMEM((panels, 2, panel_rows // 2, slice_cols), jnp.bfloat16),
            pltpu.VMEM((width, slice_cols), jnp.float32),
            dma((3 + blocks,)),
            dma((offsets, 3)),
            dma((offsets, 3)),
            dma((panels, 3)),
            dma((panels, 3)),
            dma((offsets, 3)),
            dma((2, 2)),
            dma((2,)),
            dma((2,)),
            dma((panels, 2)),
            dma((6,)),
            dma((2,)),
            dma((2,)),
        ],
        compiler_params=pltpu.CompilerParams(collective_id=1, has_side_effects=True),
    )(weight_flags, ham_flags.T, weights, hamiltonian)
    return lax.cond(
        over[0, 0] > 0,
        lambda kept, *given: gathered(*given),
        lambda kept, *given: kept,
        out, weights, weight_flags, hamiltonian, ham_flags,
    )


def solution(mesh):
    placed = (P("col", "row"), P("col", "row"), P("row", "col"), P("row", "col"))
    every_panel = mesh.shape["row"] == STEPS and mesh.shape["col"] == 2 * STEPS
    return jax.shard_map(
        packed if every_panel else shards,
        mesh=mesh, in_specs=placed, out_specs=P("row", "col"), check_vma=False,
    )
```

```python
import functools

import jax
import jax.numpy as jnp
from jax import lax
from jax.experimental import pallas as pl
from jax.experimental.pallas import tpu as pltpu
from jax.sharding import PartitionSpec as P

STEPS = 4


def from_behind(block, axis, distance):
    devices = range(lax.axis_size(axis))
    route = [((i - distance) % len(devices), i) for i in devices]
    return lax.ppermute(block, axis, route)


def from_partner(value, axis, bit):
    mask = 2**bit
    pairs = [(source, source ^ mask) for source in range(lax.axis_size(axis))]
    return lax.ppermute(value, axis, pairs)


def masked(dense_tile, flag_grid):
    row_blocks, col_blocks = flag_grid.shape
    block_edge = dense_tile.shape[0] // row_blocks
    shaped = dense_tile.reshape(row_blocks, block_edge, col_blocks, block_edge)
    retain = (flag_grid > 0)[:, None, :, None]
    return jnp.where(retain, shaped, jnp.zeros_like(shaped)).reshape(dense_tile.shape)


def aligned(operand, amount, bit_count, mover):
    for level in range(bit_count):
        moved = mover(operand, level)
        chosen = (amount >> level) % 2 == 1
        operand = jnp.where(chosen, moved, operand)
    return operand


def contract(left_part, right_part):
    return lax.dot_general(
        left_part, right_part, (((0,), (0,)), ((), ())), preferred_element_type=jnp.float32
    )


def shards(weights, weight_flags, hamiltonian, ham_flags):
    row_count = lax.axis_size("row")
    bit_count = (row_count - 1).bit_length()
    row_index = lax.axis_index("row")
    col_index = lax.axis_index("col")
    pair_index = col_index // 2
    parity = col_index % 2
    w_masked = masked(weights, weight_flags)
    h_masked = masked(hamiltonian, ham_flags)
    ham_tile = aligned(
        h_masked,
        pair_index,
        bit_count,
        lambda operand, level: from_behind(operand, "row", -(1 << level)),
    )
    w_half = aligned(
        w_masked,
        row_index,
        bit_count,
        lambda operand, level: from_behind(operand, "col", -(2 << level)),
    )
    half_rows = ham_tile.shape[0] // 2
    upper_rows = ham_tile[:half_rows]
    lower_rows = ham_tile[half_rows:]
    retained = jnp.where(parity == 0, upper_rows, lower_rows)
    handed = jnp.where(parity == 0, lower_rows, upper_rows)
    received = from_partner(handed, "col", 0)
    joined = jnp.where(
        parity == 0,
        jnp.concatenate((retained, received), 1),
        jnp.concatenate((received, retained), 1),
    )
    summed = contract(w_half, joined)
    for step_index in range(1, STEPS):
        w_half = from_behind(w_half, "col", -2)
        joined = from_behind(joined, "row", -1)
        summed = summed + contract(w_half, joined)
    half_width = summed.shape[1] // 2
    own_part = jnp.where(parity == 0, summed[:, :half_width], summed[:, half_width:])
    their_part = jnp.where(parity == 0, summed[:, half_width:], summed[:, :half_width])
    summed = own_part + from_partner(their_part, "col", 0)
    return summed.astype(jnp.bfloat16)


SHARES = (5, 3)
CHUNKS = len(SHARES)
MESH = pl.DeviceIdType.MESH


def put(source, target, sent, landed, device):
    return pltpu.make_async_remote_copy(
        src_ref=source,
        dst_ref=target,
        send_sem=sent,
        recv_sem=landed,
        device_id=device,
        device_id_type=MESH,
    )


def gather_kernel(
    panels, w_flags_hbm, h_flags_hbm, w_hbm, h_hbm, out_ref, w_flags, h_flags, w_ref, h_ref, w_buf, h_buf, total,
    loaded, w_landed, up_sent, down_sent, core_sent, h_landed, h_sent,
):
    row = lax.axis_index("row")
    col = lax.axis_index("col")
    pair = col // 2
    core = col % 2
    partner = (row, pair * 2 + 1 - core)
    above = (row, col + 2)
    below = (row, col - 2)
    beside = row + 1 - 2 * (row % 2)
    across = (row + panels // 2) % panels
    opposite = (beside + panels // 2) % panels
    has_above = pair < panels - 1
    has_below = pair > 0

    loads = [
        pltpu.make_async_copy(source, target, loaded.at[n])
        for n, (source, target) in enumerate(
            ((w_flags_hbm, w_flags), (w_hbm, w_ref), (h_flags_hbm, h_flags), (h_hbm, h_ref))
        )
    ]
    for load in loads:
        load.start()

    barrier = pltpu.get_barrier_semaphore()

    def greet(device):
        pl.semaphore_signal(barrier, inc=1, device_id=device, device_id_type=MESH)

    greet(partner)
    greet((beside, col))
    greet((across, col))

    @pl.when(has_above)
    def _():
        greet(above)

    @pl.when(has_below)
    def _():
        greet(below)

    loads[0].wait()
    loads[1].wait()
    half_rows, width = w_ref.shape
    edge = half_rows // w_flags.shape[0]
    bounds = [half_rows * sum(SHARES[:k]) // sum(SHARES) for k in range(CHUNKS + 1)]
    for r in range(w_flags.shape[0]):
        for c in range(w_flags.shape[1]):
            rows, lanes = slice(r * edge, (r + 1) * edge), slice(c * edge, (c + 1) * edge)
            block = w_ref[rows, lanes]
            kept = jnp.where(w_flags[r, c] > 0, block, jnp.zeros_like(block))
            w_buf[pair, core, rows, lanes] = kept
    pl.semaphore_wait(
        barrier, 3 + has_above.astype(jnp.int32) + has_below.astype(jnp.int32)
    )

    def piece(k):
        return slice(bounds[k], bounds[k + 1])

    def go_up(panel, k):
        slot = w_buf.at[panel, core, piece(k)]
        return put(slot, slot, up_sent.at[panel, k], w_landed.at[panel, core, k], above)

    def go_down(panel, k):
        slot = w_buf.at[panel, core, piece(k)]
        return put(slot, slot, down_sent.at[panel, k], w_landed.at[panel, core, k], below)

    def go_over(panel, k):
        slot = w_buf.at[panel, core, piece(k)]
        return put(slot, slot, core_sent.at[panel, k], w_landed.at[panel, core, k], partner)

    def arrival(panel, half, k):
        slot = w_buf.at[panel, half, piece(k)]
        return put(slot, slot, core_sent.at[panel, k], w_landed.at[panel, half, k], partner)

    def h_put(panel, half, number, device):
        slot = h_buf.at[panel, half]
        return put(slot, slot, h_sent.at[number], h_landed.at[panel, half], device)

    def each(body):
        for k in range(CHUNKS):
            body(k)

    def first_sends(k):
        @pl.when(has_above)
        def _():
            go_up(pair, k).start()

        @pl.when(has_below)
        def _():
            go_down(pair, k).start()

    each(first_sends)
    loads[2].wait()
    loads[3].wait()
    for r in range(h_flags.shape[1]):
        for c in range(h_flags.shape[0]):
            lanes = slice(c * edge, (c + 1) * edge)
            block = h_ref[r * edge:(r + 1) * edge, lanes]
            half, start = divmod(r * edge, half_rows)
            kept = jnp.where(h_flags[c, r] > 0, block, jnp.zeros_like(block))
            h_buf[row, half, start:start + edge, lanes] = kept

    h_copies = [
        h_put(row, 0, 0, (beside, col)),
        h_put(row, 1, 1, (across, col)),
        h_put(row, 1, 2, (beside, col)),
        h_put(row, 0, 3, (across, col)),
    ]
    for copy in h_copies:
        copy.start()
    each(lambda k: go_over(pair, k).start())

    def relay(distance, k):
        @pl.when(pair >= distance)
        def _():
            panel = pair - distance
            arrival(panel, core, k).wait_recv()

            @pl.when(has_above)
            def _():
                go_up(panel, k).start()

            go_over(panel, k).start()

        @pl.when(pair + distance < panels)
        def _():
            panel = pair + distance
            arrival(panel, core, k).wait_recv()

            @pl.when(has_below)
            def _():
                go_down(panel, k).start()

            go_over(panel, k).start()

    each(functools.partial(relay, 1))
    h_put(beside, 0, 0, (beside, col)).wait_recv()
    relay_across = h_put(beside, 0, 4, (across, col))
    relay_across.start()
    h_put(across, 1, 0, (beside, col)).wait_recv()
    relay_beside = h_put(across, 1, 5, (beside, col))
    relay_beside.start()
    for distance in range(2, panels - 1):
        each(functools.partial(relay, distance))
    h_put(beside, 1, 0, (beside, col)).wait_recv()
    h_put(across, 0, 0, (beside, col)).wait_recv()
    h_put(opposite, 0, 0, (beside, col)).wait_recv()
    h_put(opposite, 1, 0, (beside, col)).wait_recv()

    total[...] = jnp.zeros_like(total)
    span = 2 * half_rows

    def near_panel(step, carry):
        panel = (pair + step) % panels
        gap = panel - pair

        @pl.when((gap < panels - 1) & (gap > 1 - panels))
        def _():
            each(lambda k: arrival(panel, 1 - core, k).wait_recv())
            left = w_buf[panel].reshape(span, width)
            right = h_buf[panel].reshape(span, h_buf.shape[3])
            total[...] += contract(left, right)

        return carry

    lax.fori_loop(0, panels, near_panel, 0)

    is_end = (pair == 0) | (pair == panels - 1)

    @pl.when(is_end)
    def _():
        panel = panels - 1 - pair

        def product(half, k):
            return contract(w_buf[panel, half, piece(k)], h_buf[panel, half, piece(k)])

        for k in range(CHUNKS - 1):
            arrival(panel, core, k).wait_recv()
            go_over(panel, k).start()
            total[...] += product(core, k)
            arrival(panel, 1 - core, k).wait_recv()
            total[...] += product(1 - core, k)

        last = CHUNKS - 1
        arrival(panel, core, last).wait_recv()
        go_over(panel, last).start()
        total[...] += product(core, last)
        arrival(panel, 1 - core, last).wait_recv()
        out_ref[...] = (total[...] + product(1 - core, last)).astype(out_ref.dtype)

    @pl.when(jnp.logical_not(is_end))
    def _():
        out_ref[...] = total[...].astype(out_ref.dtype)

    for copy in h_copies + [relay_across, relay_beside]:
        copy.wait_send()

    def drain(panel, carry):
        def one(k):
            go_over(panel, k).wait_send()

            @pl.when(has_above & (panel <= pair))
            def _():
                go_up(panel, k).wait_send()

            @pl.when(has_below & (panel >= pair))
            def _():
                go_down(panel, k).wait_send()

        each(one)
        return carry

    lax.fori_loop(0, panels, drain, 0)


def gathered(weights, weight_flags, hamiltonian, ham_flags):
    panels = lax.axis_size("row")
    half_rows, width = weights.shape
    panel_rows, slice_cols = hamiltonian.shape
    dma = pltpu.SemaphoreType.DMA
    vmem = pl.BlockSpec(memory_space=pltpu.VMEM)
    hbm = pl.BlockSpec(memory_space=pltpu.HBM)
    return pl.pallas_call(
        functools.partial(gather_kernel, panels),
        out_shape=pltpu.VMEM((width, slice_cols), jnp.bfloat16),
        in_specs=[hbm] * 4,
        out_specs=vmem,
        scratch_shapes=[
            pltpu.SMEM(weight_flags.shape, weight_flags.dtype),
            pltpu.SMEM(ham_flags.shape, ham_flags.dtype),
            pltpu.VMEM(weights.shape, weights.dtype),
            pltpu.VMEM(hamiltonian.shape, hamiltonian.dtype),
            pltpu.VMEM((panels, 2, half_rows, width), jnp.bfloat16),
            pltpu.VMEM((panels, 2, panel_rows // 2, slice_cols), jnp.bfloat16),
            pltpu.VMEM((width, slice_cols), jnp.float32),
            dma((4,)),
            dma((panels, 2, CHUNKS)),
            dma((panels, CHUNKS)),
            dma((panels, CHUNKS)),
            dma((panels, CHUNKS)),
            dma((panels, 2)),
            dma((6,)),
        ],
        compiler_params=pltpu.CompilerParams(collective_id=0, has_side_effects=True),
    )(weight_flags, ham_flags, weights, hamiltonian)


def packed_kernel(
    panels, w_flags_hbm, h_flags_hbm, w_hbm, h_hbm, out_ref, over_ref,
    h_flags, flags, places, first_from, starts, totals, line_over,
    w_blocks, h_ref, same, other, late_same, late_other, from_above, from_below, to_below, to_above, w_buf, h_buf, total,
    loaded, flags_landed, flags_down, flags_up, flags_core, same_landed, other_landed, down_sent, up_sent, core_sent,
    shared_landed, shared_sent, shared_core_sent, h_landed, h_sent, over_landed, over_sent,
):
    row = lax.axis_index("row")
    col = lax.axis_index("col")
    pair = col // 2
    core = col % 2
    partner = (row, pair * 2 + 1 - core)
    above = (row, col + 2)
    below = (row, col - 2)
    beside = row + 1 - 2 * (row % 2)
    across = (row + panels // 2) % panels
    opposite = (beside + panels // 2) % panels
    top = panels - 1
    has_above = pair < top
    has_below = pair > 0
    home = top
    w_flags = flags[home].at[core]
    row_blocks, col_blocks = w_flags.shape
    blocks, edge = w_blocks.shape[0], w_blocks.shape[1]
    half_rows = row_blocks * edge
    shared = from_above.shape[0]
    part = shared // 2
    base = base_slots(blocks)
    rest = blocks - base
    slices = [slice(base * k // PIECES, base * (k + 1) // PIECES) for k in range(PIECES)]
    final_piece = slices[-1]
    WHOLE = 0
    far = top
    edges = (home - far, home + far)

    flag_load = pltpu.make_async_copy(w_flags_hbm, w_flags, loaded.at[0])
    flag_load.start()
    for b in range(blocks):
        r, c = divmod(b, col_blocks)
        source = w_hbm.at[r * edge:(r + 1) * edge, c * edge:(c + 1) * edge]
        pltpu.make_async_copy(source, w_blocks.at[b], loaded.at[3]).start()
    h_loads = [
        pltpu.make_async_copy(h_flags_hbm, h_flags, loaded.at[1]),
        pltpu.make_async_copy(h_hbm, h_ref, loaded.at[2]),
    ]
    for load in h_loads:
        load.start()

    barrier = pltpu.get_barrier_semaphore()

    def greet(device):
        pl.semaphore_signal(barrier, inc=1, device_id=device, device_id_type=MESH)

    greet(partner)
    greet((beside, col))
    greet((across, col))

    @pl.when(has_above)
    def _():
        greet(above)

    @pl.when(has_below)
    def _():
        greet(below)

    def piece(refs, late, o, k):
        if o in edges and k == PIECES - 1:
            return late[edges.index(o)]
        return refs[o].at[slices[k]]

    def mark(o):
        return (o - home) % panels - 1

    def go_down(d, k):
        source, target = (piece(same, late_same, home + n, k) for n in (d, d + 1))
        return put(source, target, down_sent.at[d], same_landed.at[mark(home + d + 1), k], below)

    def go_up(d, k):
        source, target = (piece(same, late_same, home - n, k) for n in (d, d + 1))
        return put(source, target, up_sent.at[d], same_landed.at[mark(home - d - 1), k], above)

    def go_over(o, k):
        if o == home:
            return put(same[o].at[:blocks], other[o].at[:blocks], core_sent.at[top], other_landed.at[top, 0], partner)
        source, target = piece(same, late_same, o, k), piece(other, late_other, o, k)
        return put(source, target, core_sent.at[mark(o)], other_landed.at[mark(o), k], partner)

    def flags_go_down(d):
        source, target = flags[home + d], flags[home + d + 1]
        return put(source, target, flags_down.at[d], flags_landed.at[mark(home + d + 1)], below)

    def flags_go_up(d):
        source, target = flags[home - d], flags[home - d - 1]
        return put(source, target, flags_up.at[d], flags_landed.at[mark(home - d - 1)], above)

    def flags_arrival(o):
        return put(flags[o], flags[o], flags_core.at[0], flags_landed.at[mark(o)], partner)

    def flags_cross(half):
        slot = flags[home].at[half]
        return put(slot, slot, flags_core.at[0], flags_landed.at[top], partner)

    def landed(o, k):
        slot = piece(same, late_same, o, k)
        return put(slot, slot, core_sent.at[0], same_landed.at[mark(o), k], partner)

    def crossed(o, k):
        return go_over(o, k)

    def all_pieces(o, sent):
        slot = same[o].at[:base]
        return put(slot, slot, sent, same_landed.at[0, 0], partner)

    def shared_half(ref, half):
        return ref.at[pl.ds(half * part, part)]

    def shared_down():
        return put(to_below, shared_half(from_above, core), shared_sent.at[0], shared_landed.at[0, 0], below)

    def shared_up():
        return put(to_above, shared_half(from_below, core), shared_sent.at[1], shared_landed.at[1, 0], above)

    def shared_over(side):
        slot = shared_half((from_above, from_below)[side], core)
        return put(slot, slot, shared_core_sent.at[side], shared_landed.at[side, 1], partner)

    def shared_arrival(side):
        slot = shared_half((from_above, from_below)[side], core)
        return put(slot, slot, shared_core_sent.at[side], shared_landed.at[side, 0], partner)

    def shared_crossed(side):
        slot = shared_half((from_above, from_below)[side], 1 - core)
        return put(slot, slot, shared_core_sent.at[side], shared_landed.at[side, 1], partner)

    NEAR, OVER, FAR = 0, 1, 2

    def h_put(panel, half, mark, sent, device):
        slot = h_buf.at[panel, half]
        return put(slot, slot, h_sent.at[sent], h_landed.at[mark, half], device)

    def h_wait(panel, mark, half):
        h_put(panel, half, mark, 0, (beside, col)).wait_recv()

    flag_load.wait()
    nearest = jnp.int32(blocks - 1)
    first_from[blocks] = nearest
    for b in reversed(range(blocks)):
        nearest = jnp.where(flags[home][core, b // col_blocks, b % col_blocks] > 0, b, nearest)
        first_from[b] = nearest
    pltpu.make_async_copy(same[home].at[:blocks], w_blocks, loaded.at[3]).wait()

    def pack(start, stop, chosen):
        for k in range(start, stop):
            same[home][k] = w_blocks[chosen]
            chosen = first_from[chosen + 1]
        return chosen

    chosen = pack(0, slices[0].stop, first_from[0])
    pl.semaphore_wait(
        barrier, 3 + has_above.astype(jnp.int32) + has_below.astype(jnp.int32)
    )

    def both_ways(k, down, up):
        @pl.when(down)
        def _():
            go_down(0, k).start()

        @pl.when(up)
        def _():
            go_up(0, k).start()

    both_ways(0, has_below, has_above)
    flags_cross(core).start()
    pack(slices[1].start, blocks, chosen)
    go_over(home, WHOLE).start()
    for load in h_loads:
        load.wait()
    for r in range(h_flags.shape[1]):
        for c in range(h_flags.shape[0]):
            lanes = slice(c * edge, (c + 1) * edge)
            block = h_ref[r * edge:(r + 1) * edge, lanes]
            half, start = divmod(r * edge, half_rows)
            kept = jnp.where(h_flags[c, r] > 0, block, jnp.zeros_like(block))
            h_buf[row, half, start:start + edge, lanes] = kept

    h_put(row, 0, NEAR, 0, (beside, col)).start()
    h_put(row, 1, OVER, 1, (across, col)).start()
    h_put(row, 1, NEAR, 0, (beside, col)).start()
    h_put(row, 0, OVER, 1, (across, col)).start()

    flags_cross(1 - core).wait_recv()

    @pl.when(has_below)
    def _():
        flags_go_down(0).start()

    @pl.when(has_above)
    def _():
        flags_go_up(0).start()

    for k in range(1, PIECES):
        both_ways(k, has_below & (pair < top), has_above & (pair > 0))

    def tabulate(o, which):
        half = core if which == 0 else 1 - core
        position = jnp.int32(0)
        for b in range(blocks):
            present = flags[o][half, b // col_blocks, b % col_blocks] > 0
            places[2 * o + which, b] = jnp.where(present, position, blocks)
            position = position + present.astype(jnp.int32)
        return jnp.maximum(position - base, 0)

    own_same = tabulate(home, 0)
    own_other = tabulate(home, 1)
    own_both = own_same + own_other
    same_start = jnp.where(core == 0, 0, own_other)
    other_start = jnp.where(core == 0, own_same, 0)

    def within(index, limit):
        return jnp.minimum(jnp.maximum(index, 0), limit - 1)

    def share(target, source):
        for n in range(part):
            slot = core * part + n
            in_same, in_other = slot - same_start, slot - other_start
            value = other[home][base + within(in_other, rest)]
            if source is not None:
                passed = source[within(slot - own_both, shared)]
                value = jnp.where((in_other >= 0) & (in_other < own_other), value, passed)
            mine = same[home][base + within(in_same, rest)]
            target[n] = jnp.where((in_same >= 0) & (in_same < own_same), mine, value)

    crossed(home, WHOLE).wait_recv()

    @pl.when(pair == top)
    def _():
        share(to_below, None)
        shared_down().start()
        for k in range(1, PIECES):
            go_down(0, k).start()

    @pl.when(pair == 0)
    def _():
        share(to_above, None)
        shared_up().start()
        for k in range(1, PIECES):
            go_up(0, k).start()

    def dense(o, which, panel, wanted):
        packed = (same, other)[which][o]
        half = core if which == 0 else 1 - core
        for r in wanted:
            for c in range(col_blocks):
                rows, lanes = slice(r * edge, (r + 1) * edge), slice(c * edge, (c + 1) * edge)
                w_buf[panel, half, rows, lanes] = packed[places[2 * o + which, r * col_blocks + c]]

    every_row = range(row_blocks)
    later_rows = range(1, row_blocks)
    for packed in (*same, *other):
        packed[blocks] = jnp.zeros((edge, edge), packed.dtype)
    dense(home, 0, pair, every_row)
    dense(home, 1, pair, every_row)
    total[...] = jnp.zeros_like(total)

    def forward(d, k):
        @pl.when(pair + d <= top)
        def _():
            landed(home + d, k).wait_recv()

            @pl.when(has_below)
            def _():
                go_down(d, k).start()

            go_over(home + d, k).start()

        @pl.when(pair - d >= 0)
        def _():
            landed(home - d, k).wait_recv()

            @pl.when(has_above)
            def _():
                go_up(d, k).start()

            go_over(home - d, k).start()

    def flags_on(d):
        @pl.when(pair + d <= top)
        def _():
            flags_arrival(home + d).wait_recv()

            if d < top:
                @pl.when(has_below)
                def _():
                    flags_go_down(d).start()

        @pl.when(pair - d >= 0)
        def _():
            flags_arrival(home - d).wait_recv()

            if d < top:
                @pl.when(has_above)
                def _():
                    flags_go_up(d).start()

    def middle(d, k):
        @pl.when(pair + d < top)
        def _():
            landed(home + d, k).wait_recv()

            @pl.when(has_below)
            def _():
                go_down(d, k).start()

            go_over(home + d, k).start()

        @pl.when(pair - d > 0)
        def _():
            landed(home - d, k).wait_recv()

            @pl.when(has_above)
            def _():
                go_up(d, k).start()

            go_over(home - d, k).start()

    def last(d):
        @pl.when(pair + d == top)
        def _():
            shared_arrival(0).wait_recv()
            shared_over(0).start()
            shared_crossed(0).wait_recv()

            @pl.when(has_below)
            def _():
                share(to_below, from_above)
                shared_down().start()

            for k in range(1, PIECES):
                landed(home + d, k).wait_recv()

                @pl.when(has_below)
                def _(k=k):
                    go_down(d, k).start()

                go_over(home + d, k).start()

        @pl.when(pair - d == 0)
        def _():
            shared_arrival(1).wait_recv()
            shared_over(1).start()
            shared_crossed(1).wait_recv()

            @pl.when(has_above)
            def _():
                share(to_above, from_below)
                shared_up().start()

            for k in range(1, PIECES):
                landed(home - d, k).wait_recv()

                @pl.when(has_above)
                def _(k=k):
                    go_up(d, k).start()

                go_over(home - d, k).start()

    def middles(d):
        for k in range(1, PIECES):
            middle(d, k)

    forward(1, 0)
    flags_on(1)
    middles(1)
    last(1)
    forward(2, 0)
    h_wait(beside, NEAR, 0)
    relay_across = h_put(beside, 0, FAR, 2, (across, col))
    relay_across.start()
    h_wait(across, OVER, 1)
    relay_beside = h_put(across, 1, FAR, 3, (beside, col))
    relay_beside.start()
    flags_on(2)
    middles(2)
    flags_on(3)

    totals[0] = jnp.where(pair > 0, own_both, 0)
    totals[1] = jnp.where(pair < top, own_both, 0)
    for side, way in ((0, 1), (1, -1)):
        starts[home, side] = jnp.int32(0)
        for d in range(1, panels):
            o, n = home + way * d, pair + way * d

            @pl.when((n >= 0) & (n <= top))
            def _(o=o, n=n, side=side):
                at_same, at_other = tabulate(o, 0), tabulate(o, 1)
                start = starts[home, side]
                starts[o, 0] = start + jnp.where(core == 0, 0, at_other)
                starts[o, 1] = start + jnp.where(core == 0, at_same, 0)
                starts[home, side] = start + at_same + at_other
                totals[0] += jnp.where(n > 0, at_same + at_other, 0)
                totals[1] += jnp.where(n < top, at_same + at_other, 0)

    line_over[0, 0] = jnp.maximum(totals[0] - shared, 0) + jnp.maximum(totals[1] - shared, 0)

    def agree(n, device):
        return put(line_over.at[2 * n], line_over.at[2 * n + 1], over_sent.at[n], over_landed.at[n], device)

    agree(0, (beside, col)).start()
    last(2)
    agree(0, (beside, col)).wait_recv()
    line_over[2, 0] = line_over[0, 0] + line_over[1, 0]
    agree(1, (across, col)).start()

    def fill(o, side):
        source = (from_above, from_below)[side]
        for n in range(rest):
            same[o][base + n] = source[within(starts[o, 0] + n, shared)]
            other[o][base + n] = source[within(starts[o, 1] + n, shared)]

    def spread(o, way_d):
        dense(o, 0, pair + way_d, every_row)
        dense(o, 1, pair + way_d, every_row)

    h_wait(beside, NEAR, 1)
    h_wait(across, OVER, 0)
    span = 2 * half_rows
    width = col_blocks * edge

    def add(panel):
        left = w_buf[panel].reshape(span, width)
        right = h_buf[panel].reshape(span, h_buf.shape[3])
        total[...] += contract(left, right)

    @pl.when(pair != opposite)
    def _():
        add(pair)

    sides = ((0, 1), (1, -1))

    def at_end(body):
        for side, way in sides:
            @pl.when(pair == (0, top)[side])
            def _(side=side, way=way):
                body(side, home + way * far, pair + way * far)

    def far_first(side, o, panel):
        landed(o, 0).wait_recv()
        go_over(o, 0).start()
        shared_arrival(side).wait_recv()
        shared_over(side).start()
        shared_crossed(side).wait_recv()

    at_end(far_first)

    for side, way in sides:
        for d in range(1, far):
            o, n = home + way * d, pair + way * d

            @pl.when((n >= 0) & (n <= top))
            def _(o=o, side=side, way=way, d=d):
                for k in range(PIECES):
                    crossed(o, k).wait_recv()
                fill(o, side)
                spread(o, way * d)

    def near(panel):
        gap = panel - pair
        return (gap < far) & (gap > -far)

    def near_panel(step, carry):
        panel = (pair + step) % panels

        @pl.when(near(panel) & (panel != opposite))
        def _():
            add(panel)

        return carry

    def far_middle(side, o, panel):
        for k in range(1, PIECES - 1):
            landed(o, k).wait_recv()
            go_over(o, k).start()

    at_end(far_middle)
    lax.fori_loop(1, panels, near_panel, 0)

    h_wait(opposite, FAR, 0)
    h_wait(opposite, FAR, 1)

    @pl.when(near(opposite))
    def _():
        add(opposite)

    is_end = (pair == 0) | (pair == top)

    def far_rows(side, o, panel):
        for k in range(PIECES - 1):
            crossed(o, k).wait_recv()
        fill(o, side)
        dense(o, 0, panel, range(1))
        dense(o, 1, panel, range(1))

    at_end(far_rows)

    @pl.when(is_end)
    def _():
        panel = top - pair
        left = w_buf[panel, :, :edge].reshape(2 * edge, width)
        right = h_buf[panel, :, :edge].reshape(2 * edge, h_buf.shape[3])
        total[...] += contract(left, right)

    def far_same(side, o, panel):
        landed(o, PIECES - 1).wait_recv()
        go_over(o, PIECES - 1).start()
        same[o][final_piece] = late_same[side ^ 1][...]
        dense(o, 0, panel, later_rows)

    at_end(far_same)

    @pl.when(is_end)
    def _():
        panel = top - pair
        total[...] += contract(w_buf[panel, core, edge:], h_buf[panel, core, edge:])

    def far_other(side, o, panel):
        crossed(o, PIECES - 1).wait_recv()
        other[o][final_piece] = late_other[side ^ 1][...]
        dense(o, 1, panel, later_rows)

    at_end(far_other)

    @pl.when(is_end)
    def _():
        panel = top - pair
        final = total[...] + contract(w_buf[panel, 1 - core, edge:], h_buf[panel, 1 - core, edge:])
        out_ref[...] = final.astype(out_ref.dtype)

    @pl.when(jnp.logical_not(is_end))
    def _():
        out_ref[...] = total[...].astype(out_ref.dtype)

    agree(1, (across, col)).wait_recv()
    over_ref[0, 0] = line_over[2, 0] + line_over[3, 0]
    for n in range(2):
        agree(n, (beside, col)).wait_send()
    both_halves = h_buf.at[row]
    for number, device in ((0, (beside, col)), (1, (across, col))):
        put(both_halves, both_halves, h_sent.at[number], h_landed.at[0, 0], device).wait_send()
    relay_across.wait_send()
    relay_beside.wait_send()
    flags_cross(core).wait_send()
    go_over(home, WHOLE).wait_send()

    @pl.when(has_above)
    def _():
        shared_over(0).wait_send()
        shared_up().wait_send()

    @pl.when(has_below)
    def _():
        shared_over(1).wait_send()
        shared_down().wait_send()

    for d in range(far):
        @pl.when(has_below & (pair + d <= top))
        def _(d=d):
            flags_go_down(d).wait_send()
            all_pieces(home + d, down_sent.at[d]).wait_send()

        @pl.when(has_above & (pair - d >= 0))
        def _(d=d):
            flags_go_up(d).wait_send()
            all_pieces(home - d, up_sent.at[d]).wait_send()

    for d in range(1, panels):
        @pl.when(pair + d <= top)
        def _(d=d):
            all_pieces(home + d, core_sent.at[mark(home + d)]).wait_send()

        @pl.when(pair - d >= 0)
        def _(d=d):
            all_pieces(home - d, core_sent.at[mark(home - d)]).wait_send()


def base_slots(blocks):
    return 2 * blocks // 3


PIECES = 3


def packed(weights, weight_flags, hamiltonian, ham_flags):
    weights, weight_flags, hamiltonian, ham_flags = (
        pltpu.with_memory_space_constraint(given, pltpu.HBM)
        for given in (weights, weight_flags, hamiltonian, ham_flags.T)
    )
    panels = lax.axis_size("row")
    half_rows, width = weights.shape
    panel_rows, slice_cols = hamiltonian.shape
    edge = half_rows // weight_flags.shape[0]
    blocks = weight_flags.size
    base = base_slots(blocks)
    shared = base
    offsets = 2 * panels - 1
    dma = pltpu.SemaphoreType.DMA
    hbm = pl.BlockSpec(memory_space=pltpu.HBM)

    def slots(count):
        return pltpu.VMEM((count, edge, edge), jnp.bfloat16)

    out, over = pl.pallas_call(
        functools.partial(packed_kernel, panels),
        out_shape=(
            pltpu.VMEM((width, slice_cols), jnp.bfloat16),
            jax.ShapeDtypeStruct((1, 1), jnp.int32),
        ),
        in_specs=[hbm] * 4,
        out_specs=(pl.BlockSpec(memory_space=pltpu.VMEM), pl.BlockSpec(memory_space=pltpu.SMEM)),
        scratch_shapes=[
            pltpu.SMEM(ham_flags.shape, ham_flags.dtype),
            [pltpu.SMEM((2, *weight_flags.shape), weight_flags.dtype) for _ in range(offsets)],
            pltpu.SMEM((2 * offsets, blocks), jnp.int32),
            pltpu.SMEM((blocks + 1,), jnp.int32),
            pltpu.SMEM((offsets, 2), jnp.int32),
            pltpu.SMEM((2,), jnp.int32),
            pltpu.SMEM((4, 1), jnp.int32),
            slots(blocks),
            pltpu.VMEM(hamiltonian.shape, hamiltonian.dtype),
            [slots(blocks + 1) for _ in range(offsets)],
            [slots(blocks + 1) for _ in range(offsets)],
            [slots(base // PIECES) for _ in range(2)],
            [slots(base // PIECES) for _ in range(2)],
            slots(shared),
            slots(shared),
            slots(shared // 2),
            slots(shared // 2),
            pltpu.VMEM((panels, 2, half_rows, width), jnp.bfloat16),
            pltpu.VMEM((panels, 2, panel_rows // 2, slice_cols), jnp.bfloat16),
            pltpu.VMEM((width, slice_cols), jnp.float32),
            dma((4,)),
            dma((panels,)),
            dma((panels - 1,)),
            dma((panels - 1,)),
            dma((1,)),
            dma((panels - 1, PIECES)),
            dma((panels, PIECES)),
            dma((panels - 1,)),
            dma((panels - 1,)),
            dma((panels,)),
            dma((2, 2)),
            dma((2,)),
            dma((2,)),
            dma((3, 2)),
            dma((4,)),
            dma((2,)),
            dma((2,)),
        ],
        compiler_params=pltpu.CompilerParams(collective_id=1, has_side_effects=True),
    )(weight_flags, ham_flags, weights, hamiltonian)
    return lax.cond(
        over[0, 0] > 0,
        lambda kept, *given: gathered(*given),
        lambda kept, *given: kept,
        out, weights, weight_flags, hamiltonian, ham_flags,
    )


def solution(mesh):
    placed = (P("col", "row"), P("col", "row"), P("row", "col"), P("row", "col"))
    every_panel = mesh.shape["row"] == STEPS and mesh.shape["col"] == 2 * STEPS
    return jax.shard_map(
        packed if every_panel else shards,
        mesh=mesh, in_specs=placed, out_specs=P("row", "col"), check_vma=False,
    )
```

```python
import functools

import jax
import jax.numpy as jnp
from jax import lax
from jax.experimental import pallas as pl
from jax.experimental.pallas import tpu as pltpu
from jax.sharding import PartitionSpec as P

STEPS = 4


def from_behind(block, axis, distance):
    devices = range(lax.axis_size(axis))
    route = [((i - distance) % len(devices), i) for i in devices]
    return lax.ppermute(block, axis, route)


def from_partner(value, axis, bit):
    mask = 2**bit
    pairs = [(source, source ^ mask) for source in range(lax.axis_size(axis))]
    return lax.ppermute(value, axis, pairs)


def masked(dense_tile, flag_grid):
    row_blocks, col_blocks = flag_grid.shape
    block_edge = dense_tile.shape[0] // row_blocks
    shaped = dense_tile.reshape(row_blocks, block_edge, col_blocks, block_edge)
    retain = (flag_grid > 0)[:, None, :, None]
    return jnp.where(retain, shaped, jnp.zeros_like(shaped)).reshape(dense_tile.shape)


def aligned(operand, amount, bit_count, mover):
    for level in range(bit_count):
        moved = mover(operand, level)
        chosen = (amount >> level) % 2 == 1
        operand = jnp.where(chosen, moved, operand)
    return operand


def contract(left_part, right_part):
    return lax.dot_general(
        left_part, right_part, (((0,), (0,)), ((), ())), preferred_element_type=jnp.float32
    )


def shards(weights, weight_flags, hamiltonian, ham_flags):
    row_count = lax.axis_size("row")
    bit_count = (row_count - 1).bit_length()
    row_index = lax.axis_index("row")
    col_index = lax.axis_index("col")
    pair_index = col_index // 2
    parity = col_index % 2
    w_masked = masked(weights, weight_flags)
    h_masked = masked(hamiltonian, ham_flags)
    ham_tile = aligned(
        h_masked,
        pair_index,
        bit_count,
        lambda operand, level: from_behind(operand, "row", -(1 << level)),
    )
    w_half = aligned(
        w_masked,
        row_index,
        bit_count,
        lambda operand, level: from_behind(operand, "col", -(2 << level)),
    )
    half_rows = ham_tile.shape[0] // 2
    upper_rows = ham_tile[:half_rows]
    lower_rows = ham_tile[half_rows:]
    retained = jnp.where(parity == 0, upper_rows, lower_rows)
    handed = jnp.where(parity == 0, lower_rows, upper_rows)
    received = from_partner(handed, "col", 0)
    joined = jnp.where(
        parity == 0,
        jnp.concatenate((retained, received), 1),
        jnp.concatenate((received, retained), 1),
    )
    summed = contract(w_half, joined)
    for step_index in range(1, STEPS):
        w_half = from_behind(w_half, "col", -2)
        joined = from_behind(joined, "row", -1)
        summed = summed + contract(w_half, joined)
    half_width = summed.shape[1] // 2
    own_part = jnp.where(parity == 0, summed[:, :half_width], summed[:, half_width:])
    their_part = jnp.where(parity == 0, summed[:, half_width:], summed[:, :half_width])
    summed = own_part + from_partner(their_part, "col", 0)
    return summed.astype(jnp.bfloat16)


SHARES = (5, 3)
CHUNKS = len(SHARES)
MESH = pl.DeviceIdType.MESH


def put(source, target, sent, landed, device):
    return pltpu.make_async_remote_copy(
        src_ref=source,
        dst_ref=target,
        send_sem=sent,
        recv_sem=landed,
        device_id=device,
        device_id_type=MESH,
    )


def gather_kernel(
    panels, w_flags_hbm, h_flags_hbm, w_hbm, h_hbm, out_ref, w_flags, h_flags, w_ref, h_ref, w_buf, h_buf, total,
    loaded, w_landed, up_sent, down_sent, core_sent, h_landed, h_sent,
):
    row = lax.axis_index("row")
    col = lax.axis_index("col")
    pair = col // 2
    core = col % 2
    partner = (row, pair * 2 + 1 - core)
    above = (row, col + 2)
    below = (row, col - 2)
    beside = row + 1 - 2 * (row % 2)
    across = (row + panels // 2) % panels
    opposite = (beside + panels // 2) % panels
    has_above = pair < panels - 1
    has_below = pair > 0

    loads = [
        pltpu.make_async_copy(source, target, loaded.at[n])
        for n, (source, target) in enumerate(
            ((w_flags_hbm, w_flags), (w_hbm, w_ref), (h_flags_hbm, h_flags), (h_hbm, h_ref))
        )
    ]
    for load in loads:
        load.start()

    barrier = pltpu.get_barrier_semaphore()

    def greet(device):
        pl.semaphore_signal(barrier, inc=1, device_id=device, device_id_type=MESH)

    greet(partner)
    greet((beside, col))
    greet((across, col))

    @pl.when(has_above)
    def _():
        greet(above)

    @pl.when(has_below)
    def _():
        greet(below)

    loads[0].wait()
    loads[1].wait()
    half_rows, width = w_ref.shape
    edge = half_rows // w_flags.shape[0]
    bounds = [half_rows * sum(SHARES[:k]) // sum(SHARES) for k in range(CHUNKS + 1)]
    for r in range(w_flags.shape[0]):
        for c in range(w_flags.shape[1]):
            rows, lanes = slice(r * edge, (r + 1) * edge), slice(c * edge, (c + 1) * edge)
            block = w_ref[rows, lanes]
            kept = jnp.where(w_flags[r, c] > 0, block, jnp.zeros_like(block))
            w_buf[pair, core, rows, lanes] = kept
    pl.semaphore_wait(
        barrier, 3 + has_above.astype(jnp.int32) + has_below.astype(jnp.int32)
    )

    def piece(k):
        return slice(bounds[k], bounds[k + 1])

    def go_up(panel, k):
        slot = w_buf.at[panel, core, piece(k)]
        return put(slot, slot, up_sent.at[panel, k], w_landed.at[panel, core, k], above)

    def go_down(panel, k):
        slot = w_buf.at[panel, core, piece(k)]
        return put(slot, slot, down_sent.at[panel, k], w_landed.at[panel, core, k], below)

    def go_over(panel, k):
        slot = w_buf.at[panel, core, piece(k)]
        return put(slot, slot, core_sent.at[panel, k], w_landed.at[panel, core, k], partner)

    def arrival(panel, half, k):
        slot = w_buf.at[panel, half, piece(k)]
        return put(slot, slot, core_sent.at[panel, k], w_landed.at[panel, half, k], partner)

    def h_put(panel, half, number, device):
        slot = h_buf.at[panel, half]
        return put(slot, slot, h_sent.at[number], h_landed.at[panel, half], device)

    def each(body):
        for k in range(CHUNKS):
            body(k)

    def first_sends(k):
        @pl.when(has_above)
        def _():
            go_up(pair, k).start()

        @pl.when(has_below)
        def _():
            go_down(pair, k).start()

    each(first_sends)
    loads[2].wait()
    loads[3].wait()
    for r in range(h_flags.shape[1]):
        for c in range(h_flags.shape[0]):
            lanes = slice(c * edge, (c + 1) * edge)
            block = h_ref[r * edge:(r + 1) * edge, lanes]
            half, start = divmod(r * edge, half_rows)
            kept = jnp.where(h_flags[c, r] > 0, block, jnp.zeros_like(block))
            h_buf[row, half, start:start + edge, lanes] = kept

    h_copies = [
        h_put(row, 0, 0, (beside, col)),
        h_put(row, 1, 1, (across, col)),
        h_put(row, 1, 2, (beside, col)),
        h_put(row, 0, 3, (across, col)),
    ]
    for copy in h_copies:
        copy.start()
    each(lambda k: go_over(pair, k).start())

    def relay(distance, k):
        @pl.when(pair >= distance)
        def _():
            panel = pair - distance
            arrival(panel, core, k).wait_recv()

            @pl.when(has_above)
            def _():
                go_up(panel, k).start()

            go_over(panel, k).start()

        @pl.when(pair + distance < panels)
        def _():
            panel = pair + distance
            arrival(panel, core, k).wait_recv()

            @pl.when(has_below)
            def _():
                go_down(panel, k).start()

            go_over(panel, k).start()

    each(functools.partial(relay, 1))
    h_put(beside, 0, 0, (beside, col)).wait_recv()
    relay_across = h_put(beside, 0, 4, (across, col))
    relay_across.start()
    h_put(across, 1, 0, (beside, col)).wait_recv()
    relay_beside = h_put(across, 1, 5, (beside, col))
    relay_beside.start()
    for distance in range(2, panels - 1):
        each(functools.partial(relay, distance))
    h_put(beside, 1, 0, (beside, col)).wait_recv()
    h_put(across, 0, 0, (beside, col)).wait_recv()
    h_put(opposite, 0, 0, (beside, col)).wait_recv()
    h_put(opposite, 1, 0, (beside, col)).wait_recv()

    total[...] = jnp.zeros_like(total)
    span = 2 * half_rows

    def near_panel(step, carry):
        panel = (pair + step) % panels
        gap = panel - pair

        @pl.when((gap < panels - 1) & (gap > 1 - panels))
        def _():
            each(lambda k: arrival(panel, 1 - core, k).wait_recv())
            left = w_buf[panel].reshape(span, width)
            right = h_buf[panel].reshape(span, h_buf.shape[3])
            total[...] += contract(left, right)

        return carry

    lax.fori_loop(0, panels, near_panel, 0)

    is_end = (pair == 0) | (pair == panels - 1)

    @pl.when(is_end)
    def _():
        panel = panels - 1 - pair

        def product(half, k):
            return contract(w_buf[panel, half, piece(k)], h_buf[panel, half, piece(k)])

        for k in range(CHUNKS - 1):
            arrival(panel, core, k).wait_recv()
            go_over(panel, k).start()
            total[...] += product(core, k)
            arrival(panel, 1 - core, k).wait_recv()
            total[...] += product(1 - core, k)

        last = CHUNKS - 1
        arrival(panel, core, last).wait_recv()
        go_over(panel, last).start()
        total[...] += product(core, last)
        arrival(panel, 1 - core, last).wait_recv()
        out_ref[...] = (total[...] + product(1 - core, last)).astype(out_ref.dtype)

    @pl.when(jnp.logical_not(is_end))
    def _():
        out_ref[...] = total[...].astype(out_ref.dtype)

    for copy in h_copies + [relay_across, relay_beside]:
        copy.wait_send()

    def drain(panel, carry):
        def one(k):
            go_over(panel, k).wait_send()

            @pl.when(has_above & (panel <= pair))
            def _():
                go_up(panel, k).wait_send()

            @pl.when(has_below & (panel >= pair))
            def _():
                go_down(panel, k).wait_send()

        each(one)
        return carry

    lax.fori_loop(0, panels, drain, 0)


def gathered(weights, weight_flags, hamiltonian, ham_flags):
    panels = lax.axis_size("row")
    half_rows, width = weights.shape
    panel_rows, slice_cols = hamiltonian.shape
    dma = pltpu.SemaphoreType.DMA
    vmem = pl.BlockSpec(memory_space=pltpu.VMEM)
    hbm = pl.BlockSpec(memory_space=pltpu.HBM)
    return pl.pallas_call(
        functools.partial(gather_kernel, panels),
        out_shape=pltpu.VMEM((width, slice_cols), jnp.bfloat16),
        in_specs=[hbm] * 4,
        out_specs=vmem,
        scratch_shapes=[
            pltpu.SMEM(weight_flags.shape, weight_flags.dtype),
            pltpu.SMEM(ham_flags.shape, ham_flags.dtype),
            pltpu.VMEM(weights.shape, weights.dtype),
            pltpu.VMEM(hamiltonian.shape, hamiltonian.dtype),
            pltpu.VMEM((panels, 2, half_rows, width), jnp.bfloat16),
            pltpu.VMEM((panels, 2, panel_rows // 2, slice_cols), jnp.bfloat16),
            pltpu.VMEM((width, slice_cols), jnp.float32),
            dma((4,)),
            dma((panels, 2, CHUNKS)),
            dma((panels, CHUNKS)),
            dma((panels, CHUNKS)),
            dma((panels, CHUNKS)),
            dma((panels, 2)),
            dma((6,)),
        ],
        compiler_params=pltpu.CompilerParams(collective_id=0, has_side_effects=True),
    )(weight_flags, ham_flags, weights, hamiltonian)


def packed_kernel(
    panels, w_flags_hbm, h_flags_hbm, w_hbm, h_hbm, out_ref, over_ref,
    h_flags, flags, places, first_from, starts, totals, line_over,
    w_blocks, h_ref, same, other, late_same, late_other, from_above, from_below, to_below, to_above, w_buf, h_buf, total,
    loaded, flags_landed, flags_down, flags_up, flags_core, same_landed, other_landed, down_sent, up_sent, core_sent,
    shared_landed, shared_sent, shared_core_sent, h_landed, h_sent, over_landed, over_sent,
):
    row = lax.axis_index("row")
    col = lax.axis_index("col")
    pair = col // 2
    core = col % 2
    partner = (row, pair * 2 + 1 - core)
    above = (row, col + 2)
    below = (row, col - 2)
    beside = row + 1 - 2 * (row % 2)
    across = (row + panels // 2) % panels
    opposite = (beside + panels // 2) % panels
    top = panels - 1
    has_above = pair < top
    has_below = pair > 0
    home = top
    w_flags = flags[home].at[core]
    row_blocks, col_blocks = w_flags.shape
    blocks, edge = w_blocks.shape[0], w_blocks.shape[1]
    half_rows = row_blocks * edge
    shared = from_above.shape[0]
    part = shared // 2
    base = base_slots(blocks)
    rest = blocks - base
    slices = [slice(base * k // PIECES, base * (k + 1) // PIECES) for k in range(PIECES)]
    final_piece = slices[-1]
    WHOLE = 0
    far = top
    edges = (home - far, home + far)

    flag_load = pltpu.make_async_copy(w_flags_hbm, w_flags, loaded.at[0])
    flag_load.start()
    for b in range(blocks):
        r, c = divmod(b, col_blocks)
        source = w_hbm.at[r * edge:(r + 1) * edge, c * edge:(c + 1) * edge]
        pltpu.make_async_copy(source, w_blocks.at[b], loaded.at[3]).start()
    h_loads = [
        pltpu.make_async_copy(h_flags_hbm, h_flags, loaded.at[1]),
        pltpu.make_async_copy(h_hbm, h_ref, loaded.at[2]),
    ]
    for load in h_loads:
        load.start()

    barrier = pltpu.get_barrier_semaphore()

    def greet(device):
        pl.semaphore_signal(barrier, inc=1, device_id=device, device_id_type=MESH)

    greet(partner)
    greet((beside, col))
    greet((across, col))

    @pl.when(has_above)
    def _():
        greet(above)

    @pl.when(has_below)
    def _():
        greet(below)

    def piece(refs, late, o, k):
        if o in edges and k == PIECES - 1:
            return late[edges.index(o)]
        return refs[o].at[slices[k]]

    def mark(o):
        return (o - home) % panels - 1

    def go_down(d, k):
        source, target = (piece(same, late_same, home + n, k) for n in (d, d + 1))
        return put(source, target, down_sent.at[d], same_landed.at[mark(home + d + 1), k], below)

    def go_up(d, k):
        source, target = (piece(same, late_same, home - n, k) for n in (d, d + 1))
        return put(source, target, up_sent.at[d], same_landed.at[mark(home - d - 1), k], above)

    def go_over(o, k):
        if o == home:
            return put(same[o].at[:blocks], other[o].at[:blocks], core_sent.at[top], other_landed.at[top, 0], partner)
        source, target = piece(same, late_same, o, k), piece(other, late_other, o, k)
        return put(source, target, core_sent.at[mark(o)], other_landed.at[mark(o), k], partner)

    def flags_go_down(d):
        source, target = flags[home + d], flags[home + d + 1]
        return put(source, target, flags_down.at[d], flags_landed.at[mark(home + d + 1)], below)

    def flags_go_up(d):
        source, target = flags[home - d], flags[home - d - 1]
        return put(source, target, flags_up.at[d], flags_landed.at[mark(home - d - 1)], above)

    def flags_arrival(o):
        return put(flags[o], flags[o], flags_core.at[0], flags_landed.at[mark(o)], partner)

    def flags_cross(half):
        slot = flags[home].at[half]
        return put(slot, slot, flags_core.at[0], flags_landed.at[top], partner)

    def landed(o, k):
        slot = piece(same, late_same, o, k)
        return put(slot, slot, core_sent.at[0], same_landed.at[mark(o), k], partner)

    def crossed(o, k):
        return go_over(o, k)

    def all_pieces(o, sent):
        slot = same[o].at[:base]
        return put(slot, slot, sent, same_landed.at[0, 0], partner)

    def shared_half(ref, half):
        return ref.at[pl.ds(half * part, part)]

    def shared_down():
        return put(to_below, shared_half(from_above, core), shared_sent.at[0], shared_landed.at[0, 0], below)

    def shared_up():
        return put(to_above, shared_half(from_below, core), shared_sent.at[1], shared_landed.at[1, 0], above)

    def shared_over(side):
        slot = shared_half((from_above, from_below)[side], core)
        return put(slot, slot, shared_core_sent.at[side], shared_landed.at[side, 1], partner)

    def shared_arrival(side):
        slot = shared_half((from_above, from_below)[side], core)
        return put(slot, slot, shared_core_sent.at[side], shared_landed.at[side, 0], partner)

    def shared_crossed(side):
        slot = shared_half((from_above, from_below)[side], 1 - core)
        return put(slot, slot, shared_core_sent.at[side], shared_landed.at[side, 1], partner)

    NEAR, OVER, FAR = 0, 1, 2

    def h_put(panel, half, mark, sent, device):
        slot = h_buf.at[panel, half]
        return put(slot, slot, h_sent.at[sent], h_landed.at[mark, half], device)

    def h_wait(panel, mark, half):
        h_put(panel, half, mark, 0, (beside, col)).wait_recv()

    flag_load.wait()
    nearest = jnp.int32(blocks - 1)
    first_from[blocks] = nearest
    for b in reversed(range(blocks)):
        nearest = jnp.where(flags[home][core, b // col_blocks, b % col_blocks] > 0, b, nearest)
        first_from[b] = nearest
    pltpu.make_async_copy(same[home].at[:blocks], w_blocks, loaded.at[3]).wait()

    def pack(start, stop, chosen):
        for k in range(start, stop):
            same[home][k] = w_blocks[chosen]
            chosen = first_from[chosen + 1]
        return chosen

    chosen = pack(0, slices[0].stop, first_from[0])
    pl.semaphore_wait(
        barrier, 3 + has_above.astype(jnp.int32) + has_below.astype(jnp.int32)
    )

    def both_ways(k, down, up):
        @pl.when(down)
        def _():
            go_down(0, k).start()

        @pl.when(up)
        def _():
            go_up(0, k).start()

    both_ways(0, has_below, has_above)
    flags_cross(core).start()
    pack(slices[1].start, blocks, chosen)
    go_over(home, WHOLE).start()
    for load in h_loads:
        load.wait()
    for r in range(h_flags.shape[1]):
        for c in range(h_flags.shape[0]):
            lanes = slice(c * edge, (c + 1) * edge)
            block = h_ref[r * edge:(r + 1) * edge, lanes]
            half, start = divmod(r * edge, half_rows)
            kept = jnp.where(h_flags[c, r] > 0, block, jnp.zeros_like(block))
            h_buf[row, half, start:start + edge, lanes] = kept

    h_put(row, 0, NEAR, 0, (beside, col)).start()
    h_put(row, 1, OVER, 1, (across, col)).start()
    h_put(row, 1, NEAR, 0, (beside, col)).start()
    h_put(row, 0, OVER, 1, (across, col)).start()

    flags_cross(1 - core).wait_recv()

    @pl.when(has_below)
    def _():
        flags_go_down(0).start()

    @pl.when(has_above)
    def _():
        flags_go_up(0).start()

    for k in range(1, PIECES):
        both_ways(k, has_below & (pair < top), has_above & (pair > 0))

    def tabulate(o, which):
        half = core if which == 0 else 1 - core
        position = jnp.int32(0)
        for b in range(blocks):
            present = flags[o][half, b // col_blocks, b % col_blocks] > 0
            places[2 * o + which, b] = jnp.where(present, position, blocks)
            position = position + present.astype(jnp.int32)
        return jnp.maximum(position - base, 0)

    own_same = tabulate(home, 0)
    own_other = tabulate(home, 1)
    own_both = own_same + own_other
    same_start = jnp.where(core == 0, 0, own_other)
    other_start = jnp.where(core == 0, own_same, 0)

    def within(index, limit):
        return jnp.minimum(jnp.maximum(index, 0), limit - 1)

    def share(target, source):
        for n in range(part):
            slot = core * part + n
            in_same, in_other = slot - same_start, slot - other_start
            value = other[home][base + within(in_other, rest)]
            if source is not None:
                passed = source[within(slot - own_both, shared)]
                value = jnp.where((in_other >= 0) & (in_other < own_other), value, passed)
            mine = same[home][base + within(in_same, rest)]
            target[n] = jnp.where((in_same >= 0) & (in_same < own_same), mine, value)

    crossed(home, WHOLE).wait_recv()

    @pl.when(pair == top)
    def _():
        share(to_below, None)
        shared_down().start()
        for k in range(1, PIECES):
            go_down(0, k).start()

    @pl.when(pair == 0)
    def _():
        share(to_above, None)
        shared_up().start()
        for k in range(1, PIECES):
            go_up(0, k).start()

    def dense(o, which, panel, wanted):
        packed = (same, other)[which][o]
        half = core if which == 0 else 1 - core
        for r in wanted:
            for c in range(col_blocks):
                rows, lanes = slice(r * edge, (r + 1) * edge), slice(c * edge, (c + 1) * edge)
                w_buf[panel, half, rows, lanes] = packed[places[2 * o + which, r * col_blocks + c]]

    every_row = range(row_blocks)
    later_rows = range(1, row_blocks)
    for packed in (*same, *other):
        packed[blocks] = jnp.zeros((edge, edge), packed.dtype)
    dense(home, 0, pair, every_row)
    dense(home, 1, pair, every_row)
    total[...] = jnp.zeros_like(total)
    span = 2 * half_rows
    width = col_blocks * edge

    def add(panel):
        left = w_buf[panel].reshape(span, width)
        right = h_buf[panel].reshape(span, h_buf.shape[3])
        total[...] += contract(left, right)

    @pl.when(pair == row)
    def _():
        add(pair)

    def forward(d, k):
        @pl.when(pair + d <= top)
        def _():
            landed(home + d, k).wait_recv()

            @pl.when(has_below)
            def _():
                go_down(d, k).start()

            go_over(home + d, k).start()

        @pl.when(pair - d >= 0)
        def _():
            landed(home - d, k).wait_recv()

            @pl.when(has_above)
            def _():
                go_up(d, k).start()

            go_over(home - d, k).start()

    def flags_on(d):
        @pl.when(pair + d <= top)
        def _():
            flags_arrival(home + d).wait_recv()

            if d < top:
                @pl.when(has_below)
                def _():
                    flags_go_down(d).start()

        @pl.when(pair - d >= 0)
        def _():
            flags_arrival(home - d).wait_recv()

            if d < top:
                @pl.when(has_above)
                def _():
                    flags_go_up(d).start()

    def middle(d, k):
        @pl.when(pair + d < top)
        def _():
            landed(home + d, k).wait_recv()

            @pl.when(has_below)
            def _():
                go_down(d, k).start()

            go_over(home + d, k).start()

        @pl.when(pair - d > 0)
        def _():
            landed(home - d, k).wait_recv()

            @pl.when(has_above)
            def _():
                go_up(d, k).start()

            go_over(home - d, k).start()

    def last(d):
        @pl.when(pair + d == top)
        def _():
            shared_arrival(0).wait_recv()
            shared_over(0).start()
            shared_crossed(0).wait_recv()

            @pl.when(has_below)
            def _():
                share(to_below, from_above)
                shared_down().start()

            for k in range(1, PIECES):
                landed(home + d, k).wait_recv()

                @pl.when(has_below)
                def _(k=k):
                    go_down(d, k).start()

                go_over(home + d, k).start()

        @pl.when(pair - d == 0)
        def _():
            shared_arrival(1).wait_recv()
            shared_over(1).start()
            shared_crossed(1).wait_recv()

            @pl.when(has_above)
            def _():
                share(to_above, from_below)
                shared_up().start()

            for k in range(1, PIECES):
                landed(home - d, k).wait_recv()

                @pl.when(has_above)
                def _(k=k):
                    go_up(d, k).start()

                go_over(home - d, k).start()

    def middles(d):
        for k in range(1, PIECES):
            middle(d, k)

    forward(1, 0)
    flags_on(1)
    middles(1)
    last(1)
    forward(2, 0)
    h_wait(beside, NEAR, 0)
    relay_across = h_put(beside, 0, FAR, 2, (across, col))
    relay_across.start()
    h_wait(across, OVER, 1)
    relay_beside = h_put(across, 1, FAR, 3, (beside, col))
    relay_beside.start()
    flags_on(2)
    middles(2)
    flags_on(3)

    totals[0] = jnp.where(pair > 0, own_both, 0)
    totals[1] = jnp.where(pair < top, own_both, 0)
    for side, way in ((0, 1), (1, -1)):
        starts[home, side] = jnp.int32(0)
        for d in range(1, panels):
            o, n = home + way * d, pair + way * d

            @pl.when((n >= 0) & (n <= top))
            def _(o=o, n=n, side=side):
                at_same, at_other = tabulate(o, 0), tabulate(o, 1)
                start = starts[home, side]
                starts[o, 0] = start + jnp.where(core == 0, 0, at_other)
                starts[o, 1] = start + jnp.where(core == 0, at_same, 0)
                starts[home, side] = start + at_same + at_other
                totals[0] += jnp.where(n > 0, at_same + at_other, 0)
                totals[1] += jnp.where(n < top, at_same + at_other, 0)

    line_over[0, 0] = jnp.maximum(totals[0] - shared, 0) + jnp.maximum(totals[1] - shared, 0)

    def agree(n, device):
        return put(line_over.at[2 * n], line_over.at[2 * n + 1], over_sent.at[n], over_landed.at[n], device)

    agree(0, (beside, col)).start()
    last(2)

    def fill(o, side):
        source = (from_above, from_below)[side]
        for n in range(rest):
            same[o][base + n] = source[within(starts[o, 0] + n, shared)]
            other[o][base + n] = source[within(starts[o, 1] + n, shared)]

    def spread(o, way_d):
        dense(o, 0, pair + way_d, every_row)
        dense(o, 1, pair + way_d, every_row)

    h_wait(beside, NEAR, 1)
    h_wait(across, OVER, 0)
    @pl.when((pair != row) & (pair != opposite))
    def _():
        add(pair)

    sides = ((0, 1), (1, -1))

    def at_end(body):
        for side, way in sides:
            @pl.when(pair == (0, top)[side])
            def _(side=side, way=way):
                body(side, home + way * far, pair + way * far)

    def far_first(side, o, panel):
        landed(o, 0).wait_recv()
        go_over(o, 0).start()
        shared_arrival(side).wait_recv()
        shared_over(side).start()
        shared_crossed(side).wait_recv()

    at_end(far_first)
    agree(0, (beside, col)).wait_recv()
    line_over[2, 0] = line_over[0, 0] + line_over[1, 0]
    agree(1, (across, col)).start()

    for side, way in sides:
        for d in range(1, far):
            o, n = home + way * d, pair + way * d

            @pl.when((n >= 0) & (n <= top))
            def _(o=o, side=side, way=way, d=d):
                for k in range(PIECES):
                    crossed(o, k).wait_recv()
                fill(o, side)
                spread(o, way * d)

    def near(panel):
        gap = panel - pair
        return (gap < far) & (gap > -far)

    def near_panel(step, carry):
        panel = (pair + step) % panels

        @pl.when(near(panel) & (panel != opposite))
        def _():
            add(panel)

        return carry

    def far_middle(side, o, panel):
        for k in range(1, PIECES - 1):
            landed(o, k).wait_recv()
            go_over(o, k).start()

    at_end(far_middle)
    lax.fori_loop(1, panels, near_panel, 0)

    h_wait(opposite, FAR, 0)
    h_wait(opposite, FAR, 1)

    @pl.when(near(opposite))
    def _():
        add(opposite)

    is_end = (pair == 0) | (pair == top)

    def far_rows(side, o, panel):
        for k in range(PIECES - 1):
            crossed(o, k).wait_recv()
        fill(o, side)
        dense(o, 0, panel, range(1))
        dense(o, 1, panel, range(1))

    at_end(far_rows)

    @pl.when(is_end)
    def _():
        panel = top - pair
        left = w_buf[panel, :, :edge].reshape(2 * edge, width)
        right = h_buf[panel, :, :edge].reshape(2 * edge, h_buf.shape[3])
        total[...] += contract(left, right)

    def far_same(side, o, panel):
        landed(o, PIECES - 1).wait_recv()
        go_over(o, PIECES - 1).start()
        same[o][final_piece] = late_same[side ^ 1][...]
        dense(o, 0, panel, later_rows)

    at_end(far_same)

    @pl.when(is_end)
    def _():
        panel = top - pair
        total[...] += contract(w_buf[panel, core, edge:], h_buf[panel, core, edge:])

    def far_other(side, o, panel):
        crossed(o, PIECES - 1).wait_recv()
        other[o][final_piece] = late_other[side ^ 1][...]
        dense(o, 1, panel, later_rows)

    at_end(far_other)

    @pl.when(is_end)
    def _():
        panel = top - pair
        final = total[...] + contract(w_buf[panel, 1 - core, edge:], h_buf[panel, 1 - core, edge:])
        out_ref[...] = final.astype(out_ref.dtype)

    @pl.when(jnp.logical_not(is_end))
    def _():
        out_ref[...] = total[...].astype(out_ref.dtype)

    agree(1, (across, col)).wait_recv()
    over_ref[0, 0] = line_over[2, 0] + line_over[3, 0]
    for n in range(2):
        agree(n, (beside, col)).wait_send()
    both_halves = h_buf.at[row]
    for number, device in ((0, (beside, col)), (1, (across, col))):
        put(both_halves, both_halves, h_sent.at[number], h_landed.at[0, 0], device).wait_send()
    relay_across.wait_send()
    relay_beside.wait_send()
    flags_cross(core).wait_send()
    go_over(home, WHOLE).wait_send()

    @pl.when(has_above)
    def _():
        shared_over(0).wait_send()
        shared_up().wait_send()

    @pl.when(has_below)
    def _():
        shared_over(1).wait_send()
        shared_down().wait_send()

    for d in range(far):
        @pl.when(has_below & (pair + d <= top))
        def _(d=d):
            flags_go_down(d).wait_send()
            all_pieces(home + d, down_sent.at[d]).wait_send()

        @pl.when(has_above & (pair - d >= 0))
        def _(d=d):
            flags_go_up(d).wait_send()
            all_pieces(home - d, up_sent.at[d]).wait_send()

    for d in range(1, panels):
        @pl.when(pair + d <= top)
        def _(d=d):
            all_pieces(home + d, core_sent.at[mark(home + d)]).wait_send()

        @pl.when(pair - d >= 0)
        def _(d=d):
            all_pieces(home - d, core_sent.at[mark(home - d)]).wait_send()


def base_slots(blocks):
    return 2 * blocks // 3


PIECES = 3


def packed(weights, weight_flags, hamiltonian, ham_flags):
    weights, weight_flags, hamiltonian, ham_flags = (
        pltpu.with_memory_space_constraint(given, pltpu.HBM)
        for given in (weights, weight_flags, hamiltonian, ham_flags.T)
    )
    panels = lax.axis_size("row")
    half_rows, width = weights.shape
    panel_rows, slice_cols = hamiltonian.shape
    edge = half_rows // weight_flags.shape[0]
    blocks = weight_flags.size
    base = base_slots(blocks)
    shared = base
    offsets = 2 * panels - 1
    dma = pltpu.SemaphoreType.DMA
    hbm = pl.BlockSpec(memory_space=pltpu.HBM)

    def slots(count):
        return pltpu.VMEM((count, edge, edge), jnp.bfloat16)

    out, over = pl.pallas_call(
        functools.partial(packed_kernel, panels),
        out_shape=(
            pltpu.VMEM((width, slice_cols), jnp.bfloat16),
            pltpu.SMEM((1, 1), jnp.int32),
        ),
        in_specs=[hbm] * 4,
        out_specs=(pl.BlockSpec(memory_space=pltpu.VMEM), pl.BlockSpec(memory_space=pltpu.SMEM)),
        scratch_shapes=[
            pltpu.SMEM(ham_flags.shape, ham_flags.dtype),
            [pltpu.SMEM((2, *weight_flags.shape), weight_flags.dtype) for _ in range(offsets)],
            pltpu.SMEM((2 * offsets, blocks), jnp.int32),
            pltpu.SMEM((blocks + 1,), jnp.int32),
            pltpu.SMEM((offsets, 2), jnp.int32),
            pltpu.SMEM((2,), jnp.int32),
            pltpu.SMEM((4, 1), jnp.int32),
            slots(blocks),
            pltpu.VMEM(hamiltonian.shape, hamiltonian.dtype),
            [slots(blocks + 1) for _ in range(offsets)],
            [slots(blocks + 1) for _ in range(offsets)],
            [slots(base // PIECES) for _ in range(2)],
            [slots(base // PIECES) for _ in range(2)],
            slots(shared),
            slots(shared),
            slots(shared // 2),
            slots(shared // 2),
            pltpu.VMEM((panels, 2, half_rows, width), jnp.bfloat16),
            pltpu.VMEM((panels, 2, panel_rows // 2, slice_cols), jnp.bfloat16),
            pltpu.VMEM((width, slice_cols), jnp.float32),
            dma((4,)),
            dma((panels,)),
            dma((panels - 1,)),
            dma((panels - 1,)),
            dma((1,)),
            dma((panels - 1, PIECES)),
            dma((panels, PIECES)),
            dma((panels - 1,)),
            dma((panels - 1,)),
            dma((panels,)),
            dma((2, 2)),
            dma((2,)),
            dma((2,)),
            dma((3, 2)),
            dma((4,)),
            dma((2,)),
            dma((2,)),
        ],
        compiler_params=pltpu.CompilerParams(collective_id=1, has_side_effects=True),
    )(weight_flags, ham_flags, weights, hamiltonian)
    return lax.cond(
        over[0, 0] > 0,
        lambda kept, *given: gathered(*given),
        lambda kept, *given: kept,
        out, weights, weight_flags, hamiltonian, ham_flags,
    )


def solution(mesh):
    placed = (P("col", "row"), P("col", "row"), P("row", "col"), P("row", "col"))
    every_panel = mesh.shape["row"] == STEPS and mesh.shape["col"] == 2 * STEPS
    return jax.shard_map(
        packed if every_panel else shards,
        mesh=mesh, in_specs=placed, out_specs=P("row", "col"), check_vma=False,
    )
```

```python
import functools

import jax
import jax.numpy as jnp
from jax import lax
from jax.experimental import pallas as pl
from jax.experimental.pallas import tpu as pltpu
from jax.sharding import PartitionSpec as P

STEPS = 4


def from_behind(block, axis, distance):
    devices = range(lax.axis_size(axis))
    route = [((i - distance) % len(devices), i) for i in devices]
    return lax.ppermute(block, axis, route)


def from_partner(value, axis, bit):
    mask = 2**bit
    pairs = [(source, source ^ mask) for source in range(lax.axis_size(axis))]
    return lax.ppermute(value, axis, pairs)


def masked(dense_tile, flag_grid):
    row_blocks, col_blocks = flag_grid.shape
    block_edge = dense_tile.shape[0] // row_blocks
    shaped = dense_tile.reshape(row_blocks, block_edge, col_blocks, block_edge)
    retain = (flag_grid > 0)[:, None, :, None]
    return jnp.where(retain, shaped, jnp.zeros_like(shaped)).reshape(dense_tile.shape)


def aligned(operand, amount, bit_count, mover):
    for level in range(bit_count):
        moved = mover(operand, level)
        chosen = (amount >> level) % 2 == 1
        operand = jnp.where(chosen, moved, operand)
    return operand


def contract(left_part, right_part):
    return lax.dot_general(
        left_part, right_part, (((0,), (0,)), ((), ())), preferred_element_type=jnp.float32
    )


def shards(weights, weight_flags, hamiltonian, ham_flags):
    row_count = lax.axis_size("row")
    bit_count = (row_count - 1).bit_length()
    row_index = lax.axis_index("row")
    col_index = lax.axis_index("col")
    pair_index = col_index // 2
    parity = col_index % 2
    w_masked = masked(weights, weight_flags)
    h_masked = masked(hamiltonian, ham_flags)
    ham_tile = aligned(
        h_masked,
        pair_index,
        bit_count,
        lambda operand, level: from_behind(operand, "row", -(1 << level)),
    )
    w_half = aligned(
        w_masked,
        row_index,
        bit_count,
        lambda operand, level: from_behind(operand, "col", -(2 << level)),
    )
    half_rows = ham_tile.shape[0] // 2
    upper_rows = ham_tile[:half_rows]
    lower_rows = ham_tile[half_rows:]
    retained = jnp.where(parity == 0, upper_rows, lower_rows)
    handed = jnp.where(parity == 0, lower_rows, upper_rows)
    received = from_partner(handed, "col", 0)
    joined = jnp.where(
        parity == 0,
        jnp.concatenate((retained, received), 1),
        jnp.concatenate((received, retained), 1),
    )
    summed = contract(w_half, joined)
    for step_index in range(1, STEPS):
        w_half = from_behind(w_half, "col", -2)
        joined = from_behind(joined, "row", -1)
        summed = summed + contract(w_half, joined)
    half_width = summed.shape[1] // 2
    own_part = jnp.where(parity == 0, summed[:, :half_width], summed[:, half_width:])
    their_part = jnp.where(parity == 0, summed[:, half_width:], summed[:, :half_width])
    summed = own_part + from_partner(their_part, "col", 0)
    return summed.astype(jnp.bfloat16)


SHARES = (5, 3)
CHUNKS = len(SHARES)
MESH = pl.DeviceIdType.MESH


def put(source, target, sent, landed, device):
    return pltpu.make_async_remote_copy(
        src_ref=source,
        dst_ref=target,
        send_sem=sent,
        recv_sem=landed,
        device_id=device,
        device_id_type=MESH,
    )


def gather_kernel(
    panels, w_flags_hbm, h_flags_hbm, w_hbm, h_hbm, out_ref, w_flags, h_flags, w_ref, h_ref, w_buf, h_buf, total,
    loaded, w_landed, up_sent, down_sent, core_sent, h_landed, h_sent,
):
    row = lax.axis_index("row")
    col = lax.axis_index("col")
    pair = col // 2
    core = col % 2
    partner = (row, pair * 2 + 1 - core)
    above = (row, col + 2)
    below = (row, col - 2)
    beside = row + 1 - 2 * (row % 2)
    across = (row + panels // 2) % panels
    opposite = (beside + panels // 2) % panels
    has_above = pair < panels - 1
    has_below = pair > 0

    loads = [
        pltpu.make_async_copy(source, target, loaded.at[n])
        for n, (source, target) in enumerate(
            ((w_flags_hbm, w_flags), (w_hbm, w_ref), (h_flags_hbm, h_flags), (h_hbm, h_ref))
        )
    ]
    for load in loads:
        load.start()

    barrier = pltpu.get_barrier_semaphore()

    def greet(device):
        pl.semaphore_signal(barrier, inc=1, device_id=device, device_id_type=MESH)

    greet(partner)
    greet((beside, col))
    greet((across, col))

    @pl.when(has_above)
    def _():
        greet(above)

    @pl.when(has_below)
    def _():
        greet(below)

    loads[0].wait()
    loads[1].wait()
    half_rows, width = w_ref.shape
    edge = half_rows // w_flags.shape[0]
    bounds = [half_rows * sum(SHARES[:k]) // sum(SHARES) for k in range(CHUNKS + 1)]
    for r in range(w_flags.shape[0]):
        for c in range(w_flags.shape[1]):
            rows, lanes = slice(r * edge, (r + 1) * edge), slice(c * edge, (c + 1) * edge)
            block = w_ref[rows, lanes]
            kept = jnp.where(w_flags[r, c] > 0, block, jnp.zeros_like(block))
            w_buf[pair, core, rows, lanes] = kept
    pl.semaphore_wait(
        barrier, 3 + has_above.astype(jnp.int32) + has_below.astype(jnp.int32)
    )

    def piece(k):
        return slice(bounds[k], bounds[k + 1])

    def go_up(panel, k):
        slot = w_buf.at[panel, core, piece(k)]
        return put(slot, slot, up_sent.at[panel, k], w_landed.at[panel, core, k], above)

    def go_down(panel, k):
        slot = w_buf.at[panel, core, piece(k)]
        return put(slot, slot, down_sent.at[panel, k], w_landed.at[panel, core, k], below)

    def go_over(panel, k):
        slot = w_buf.at[panel, core, piece(k)]
        return put(slot, slot, core_sent.at[panel, k], w_landed.at[panel, core, k], partner)

    def arrival(panel, half, k):
        slot = w_buf.at[panel, half, piece(k)]
        return put(slot, slot, core_sent.at[panel, k], w_landed.at[panel, half, k], partner)

    def h_put(panel, half, number, device):
        slot = h_buf.at[panel, half]
        return put(slot, slot, h_sent.at[number], h_landed.at[panel, half], device)

    def each(body):
        for k in range(CHUNKS):
            body(k)

    def first_sends(k):
        @pl.when(has_above)
        def _():
            go_up(pair, k).start()

        @pl.when(has_below)
        def _():
            go_down(pair, k).start()

    each(first_sends)
    loads[2].wait()
    loads[3].wait()
    for r in range(h_flags.shape[1]):
        for c in range(h_flags.shape[0]):
            lanes = slice(c * edge, (c + 1) * edge)
            block = h_ref[r * edge:(r + 1) * edge, lanes]
            half, start = divmod(r * edge, half_rows)
            kept = jnp.where(h_flags[c, r] > 0, block, jnp.zeros_like(block))
            h_buf[row, half, start:start + edge, lanes] = kept

    h_copies = [
        h_put(row, 0, 0, (beside, col)),
        h_put(row, 1, 1, (across, col)),
        h_put(row, 1, 2, (beside, col)),
        h_put(row, 0, 3, (across, col)),
    ]
    for copy in h_copies:
        copy.start()
    each(lambda k: go_over(pair, k).start())

    def relay(distance, k):
        @pl.when(pair >= distance)
        def _():
            panel = pair - distance
            arrival(panel, core, k).wait_recv()

            @pl.when(has_above)
            def _():
                go_up(panel, k).start()

            go_over(panel, k).start()

        @pl.when(pair + distance < panels)
        def _():
            panel = pair + distance
            arrival(panel, core, k).wait_recv()

            @pl.when(has_below)
            def _():
                go_down(panel, k).start()

            go_over(panel, k).start()

    each(functools.partial(relay, 1))
    h_put(beside, 0, 0, (beside, col)).wait_recv()
    relay_across = h_put(beside, 0, 4, (across, col))
    relay_across.start()
    h_put(across, 1, 0, (beside, col)).wait_recv()
    relay_beside = h_put(across, 1, 5, (beside, col))
    relay_beside.start()
    for distance in range(2, panels - 1):
        each(functools.partial(relay, distance))
    h_put(beside, 1, 0, (beside, col)).wait_recv()
    h_put(across, 0, 0, (beside, col)).wait_recv()
    h_put(opposite, 0, 0, (beside, col)).wait_recv()
    h_put(opposite, 1, 0, (beside, col)).wait_recv()

    total[...] = jnp.zeros_like(total)
    span = 2 * half_rows

    def near_panel(step, carry):
        panel = (pair + step) % panels
        gap = panel - pair

        @pl.when((gap < panels - 1) & (gap > 1 - panels))
        def _():
            each(lambda k: arrival(panel, 1 - core, k).wait_recv())
            left = w_buf[panel].reshape(span, width)
            right = h_buf[panel].reshape(span, h_buf.shape[3])
            total[...] += contract(left, right)

        return carry

    lax.fori_loop(0, panels, near_panel, 0)

    is_end = (pair == 0) | (pair == panels - 1)

    @pl.when(is_end)
    def _():
        panel = panels - 1 - pair

        def product(half, k):
            return contract(w_buf[panel, half, piece(k)], h_buf[panel, half, piece(k)])

        for k in range(CHUNKS - 1):
            arrival(panel, core, k).wait_recv()
            go_over(panel, k).start()
            total[...] += product(core, k)
            arrival(panel, 1 - core, k).wait_recv()
            total[...] += product(1 - core, k)

        last = CHUNKS - 1
        arrival(panel, core, last).wait_recv()
        go_over(panel, last).start()
        total[...] += product(core, last)
        arrival(panel, 1 - core, last).wait_recv()
        out_ref[...] = (total[...] + product(1 - core, last)).astype(out_ref.dtype)

    @pl.when(jnp.logical_not(is_end))
    def _():
        out_ref[...] = total[...].astype(out_ref.dtype)

    for copy in h_copies + [relay_across, relay_beside]:
        copy.wait_send()

    def drain(panel, carry):
        def one(k):
            go_over(panel, k).wait_send()

            @pl.when(has_above & (panel <= pair))
            def _():
                go_up(panel, k).wait_send()

            @pl.when(has_below & (panel >= pair))
            def _():
                go_down(panel, k).wait_send()

        each(one)
        return carry

    lax.fori_loop(0, panels, drain, 0)


def gathered(weights, weight_flags, hamiltonian, ham_flags):
    panels = lax.axis_size("row")
    half_rows, width = weights.shape
    panel_rows, slice_cols = hamiltonian.shape
    dma = pltpu.SemaphoreType.DMA
    vmem = pl.BlockSpec(memory_space=pltpu.VMEM)
    hbm = pl.BlockSpec(memory_space=pltpu.HBM)
    return pl.pallas_call(
        functools.partial(gather_kernel, panels),
        out_shape=pltpu.VMEM((width, slice_cols), jnp.bfloat16),
        in_specs=[hbm] * 4,
        out_specs=vmem,
        scratch_shapes=[
            pltpu.SMEM(weight_flags.shape, weight_flags.dtype),
            pltpu.SMEM(ham_flags.shape, ham_flags.dtype),
            pltpu.VMEM(weights.shape, weights.dtype),
            pltpu.VMEM(hamiltonian.shape, hamiltonian.dtype),
            pltpu.VMEM((panels, 2, half_rows, width), jnp.bfloat16),
            pltpu.VMEM((panels, 2, panel_rows // 2, slice_cols), jnp.bfloat16),
            pltpu.VMEM((width, slice_cols), jnp.float32),
            dma((4,)),
            dma((panels, 2, CHUNKS)),
            dma((panels, CHUNKS)),
            dma((panels, CHUNKS)),
            dma((panels, CHUNKS)),
            dma((panels, 2)),
            dma((6,)),
        ],
        compiler_params=pltpu.CompilerParams(collective_id=0, has_side_effects=True),
    )(weight_flags, ham_flags, weights, hamiltonian)


def packed_kernel(
    panels, w_flags_hbm, h_flags_hbm, w_hbm, h_hbm, out_ref, over_ref,
    h_flags, flags, places, first_from, starts, totals, line_over,
    w_blocks, h_ref, same, other, late_same, late_other, from_above, from_below, to_below, to_above, w_buf, h_buf, total,
    loaded, flags_landed, flags_down, flags_up, flags_core, same_landed, other_landed, down_sent, up_sent, core_sent,
    shared_landed, shared_sent, shared_core_sent, h_landed, h_sent, over_landed, over_sent,
):
    row = lax.axis_index("row")
    col = lax.axis_index("col")
    pair = col // 2
    core = col % 2
    partner = (row, pair * 2 + 1 - core)
    above = (row, col + 2)
    below = (row, col - 2)
    beside = row + 1 - 2 * (row % 2)
    across = (row + panels // 2) % panels
    opposite = (beside + panels // 2) % panels
    top = panels - 1
    has_above = pair < top
    has_below = pair > 0
    home = top
    w_flags = flags[home].at[core]
    row_blocks, col_blocks = w_flags.shape
    blocks, edge = w_blocks.shape[0], w_blocks.shape[1]
    half_rows = row_blocks * edge
    shared = from_above.shape[0]
    part = shared // 2
    base = base_slots(blocks)
    rest = blocks - base
    cuts = piece_cuts(base)
    slices = [slice(*cuts[k:k + 2]) for k in range(PIECES)]
    final_piece = slices[-1]
    WHOLE = 0
    far = top
    edges = (home - far, home + far)

    flag_load = pltpu.make_async_copy(w_flags_hbm, w_flags, loaded.at[0])
    flag_load.start()
    for b in range(blocks):
        r, c = divmod(b, col_blocks)
        source = w_hbm.at[r * edge:(r + 1) * edge, c * edge:(c + 1) * edge]
        pltpu.make_async_copy(source, w_blocks.at[b], loaded.at[3]).start()
    h_loads = [
        pltpu.make_async_copy(h_flags_hbm, h_flags, loaded.at[1]),
        pltpu.make_async_copy(h_hbm, h_ref, loaded.at[2]),
    ]
    for load in h_loads:
        load.start()

    barrier = pltpu.get_barrier_semaphore()

    def greet(device):
        pl.semaphore_signal(barrier, inc=1, device_id=device, device_id_type=MESH)

    greet(partner)
    greet((beside, col))
    greet((across, col))

    @pl.when(has_above)
    def _():
        greet(above)

    @pl.when(has_below)
    def _():
        greet(below)

    def piece(refs, late, o, k):
        if o in edges and k == PIECES - 1:
            return late[edges.index(o)]
        return refs[o].at[slices[k]]

    def mark(o):
        return (o - home) % panels - 1

    def go_down(d, k):
        source, target = (piece(same, late_same, home + n, k) for n in (d, d + 1))
        return put(source, target, down_sent.at[d], same_landed.at[mark(home + d + 1), k], below)

    def go_up(d, k):
        source, target = (piece(same, late_same, home - n, k) for n in (d, d + 1))
        return put(source, target, up_sent.at[d], same_landed.at[mark(home - d - 1), k], above)

    def go_over(o, k):
        if o == home:
            return put(same[o].at[:blocks], other[o].at[:blocks], core_sent.at[top], other_landed.at[top, 0], partner)
        source, target = piece(same, late_same, o, k), piece(other, late_other, o, k)
        return put(source, target, core_sent.at[mark(o)], other_landed.at[mark(o), k], partner)

    def flags_go_down(d):
        source, target = flags[home + d], flags[home + d + 1]
        return put(source, target, flags_down.at[d], flags_landed.at[mark(home + d + 1)], below)

    def flags_go_up(d):
        source, target = flags[home - d], flags[home - d - 1]
        return put(source, target, flags_up.at[d], flags_landed.at[mark(home - d - 1)], above)

    def flags_arrival(o):
        return put(flags[o], flags[o], flags_core.at[0], flags_landed.at[mark(o)], partner)

    def flags_cross(half):
        slot = flags[home].at[half]
        return put(slot, slot, flags_core.at[0], flags_landed.at[top], partner)

    def landed(o, k):
        slot = piece(same, late_same, o, k)
        return put(slot, slot, core_sent.at[0], same_landed.at[mark(o), k], partner)

    def crossed(o, k):
        return go_over(o, k)

    def all_pieces(o, sent):
        slot = same[o].at[:base]
        return put(slot, slot, sent, same_landed.at[0, 0], partner)

    def shared_half(ref, half):
        return ref.at[pl.ds(half * part, part)]

    def shared_down():
        return put(to_below, shared_half(from_above, core), shared_sent.at[0], shared_landed.at[0, 0], below)

    def shared_up():
        return put(to_above, shared_half(from_below, core), shared_sent.at[1], shared_landed.at[1, 0], above)

    def shared_over(side):
        slot = shared_half((from_above, from_below)[side], core)
        return put(slot, slot, shared_core_sent.at[side], shared_landed.at[side, 1], partner)

    def shared_arrival(side):
        slot = shared_half((from_above, from_below)[side], core)
        return put(slot, slot, shared_core_sent.at[side], shared_landed.at[side, 0], partner)

    def shared_crossed(side):
        slot = shared_half((from_above, from_below)[side], 1 - core)
        return put(slot, slot, shared_core_sent.at[side], shared_landed.at[side, 1], partner)

    NEAR, OVER, FAR = 0, 1, 2

    def h_put(panel, half, mark, sent, device):
        slot = h_buf.at[panel, half]
        return put(slot, slot, h_sent.at[sent], h_landed.at[mark, half], device)

    def h_wait(panel, mark, half):
        h_put(panel, half, mark, 0, (beside, col)).wait_recv()

    flag_load.wait()
    nearest = jnp.int32(blocks - 1)
    first_from[blocks] = nearest
    for b in reversed(range(blocks)):
        nearest = jnp.where(flags[home][core, b // col_blocks, b % col_blocks] > 0, b, nearest)
        first_from[b] = nearest
    pltpu.make_async_copy(same[home].at[:blocks], w_blocks, loaded.at[3]).wait()

    def pack(start, stop, chosen):
        for k in range(start, stop):
            same[home][k] = w_blocks[chosen]
            chosen = first_from[chosen + 1]
        return chosen

    chosen = pack(0, slices[0].stop, first_from[0])
    pl.semaphore_wait(
        barrier, 3 + has_above.astype(jnp.int32) + has_below.astype(jnp.int32)
    )

    def both_ways(k, down, up):
        @pl.when(down)
        def _():
            go_down(0, k).start()

        @pl.when(up)
        def _():
            go_up(0, k).start()

    both_ways(0, has_below, has_above)
    flags_cross(core).start()
    pack(slices[1].start, blocks, chosen)
    go_over(home, WHOLE).start()
    for load in h_loads:
        load.wait()
    for r in range(h_flags.shape[1]):
        for c in range(h_flags.shape[0]):
            lanes = slice(c * edge, (c + 1) * edge)
            block = h_ref[r * edge:(r + 1) * edge, lanes]
            half, start = divmod(r * edge, half_rows)
            kept = jnp.where(h_flags[c, r] > 0, block, jnp.zeros_like(block))
            h_buf[row, half, start:start + edge, lanes] = kept

    h_put(row, 0, NEAR, 0, (beside, col)).start()
    h_put(row, 1, OVER, 1, (across, col)).start()
    h_put(row, 1, NEAR, 0, (beside, col)).start()
    h_put(row, 0, OVER, 1, (across, col)).start()

    flags_cross(1 - core).wait_recv()

    @pl.when(has_below)
    def _():
        flags_go_down(0).start()

    @pl.when(has_above)
    def _():
        flags_go_up(0).start()

    for k in range(1, PIECES):
        both_ways(k, has_below & (pair < top), has_above & (pair > 0))

    def tabulate(o, which):
        half = core if which == 0 else 1 - core
        position = jnp.int32(0)
        for b in range(blocks):
            present = flags[o][half, b // col_blocks, b % col_blocks] > 0
            places[2 * o + which, b] = jnp.where(present, position, blocks)
            position = position + present.astype(jnp.int32)
        return jnp.maximum(position - base, 0)

    own_same = tabulate(home, 0)
    own_other = tabulate(home, 1)
    own_both = own_same + own_other
    same_start = jnp.where(core == 0, 0, own_other)
    other_start = jnp.where(core == 0, own_same, 0)

    def within(index, limit):
        return jnp.minimum(jnp.maximum(index, 0), limit - 1)

    def share(target, source):
        for n in range(part):
            slot = core * part + n
            in_same, in_other = slot - same_start, slot - other_start
            value = other[home][base + within(in_other, rest)]
            if source is not None:
                passed = source[within(slot - own_both, shared)]
                value = jnp.where((in_other >= 0) & (in_other < own_other), value, passed)
            mine = same[home][base + within(in_same, rest)]
            target[n] = jnp.where((in_same >= 0) & (in_same < own_same), mine, value)

    crossed(home, WHOLE).wait_recv()

    @pl.when(pair == top)
    def _():
        share(to_below, None)
        shared_down().start()
        for k in range(1, PIECES):
            go_down(0, k).start()

    @pl.when(pair == 0)
    def _():
        share(to_above, None)
        shared_up().start()
        for k in range(1, PIECES):
            go_up(0, k).start()

    def dense(o, which, panel, wanted):
        packed = (same, other)[which][o]
        half = core if which == 0 else 1 - core
        for r in wanted:
            for c in range(col_blocks):
                rows, lanes = slice(r * edge, (r + 1) * edge), slice(c * edge, (c + 1) * edge)
                w_buf[panel, half, rows, lanes] = packed[places[2 * o + which, r * col_blocks + c]]

    every_row = range(row_blocks)
    later_rows = range(1, row_blocks)
    for packed in (*same, *other):
        packed[blocks] = jnp.zeros((edge, edge), packed.dtype)
    dense(home, 0, pair, every_row)
    dense(home, 1, pair, every_row)
    total[...] = jnp.zeros_like(total)
    span = 2 * half_rows
    width = col_blocks * edge

    def add(panel):
        left = w_buf[panel].reshape(span, width)
        right = h_buf[panel].reshape(span, h_buf.shape[3])
        total[...] += contract(left, right)

    @pl.when(pair == row)
    def _():
        add(pair)

    def forward(d, k):
        @pl.when(pair + d <= top)
        def _():
            landed(home + d, k).wait_recv()

            @pl.when(has_below)
            def _():
                go_down(d, k).start()

            go_over(home + d, k).start()

        @pl.when(pair - d >= 0)
        def _():
            landed(home - d, k).wait_recv()

            @pl.when(has_above)
            def _():
                go_up(d, k).start()

            go_over(home - d, k).start()

    def flags_on(d):
        @pl.when(pair + d <= top)
        def _():
            flags_arrival(home + d).wait_recv()

            if d < top:
                @pl.when(has_below)
                def _():
                    flags_go_down(d).start()

        @pl.when(pair - d >= 0)
        def _():
            flags_arrival(home - d).wait_recv()

            if d < top:
                @pl.when(has_above)
                def _():
                    flags_go_up(d).start()

    def middle(d, k):
        @pl.when(pair + d < top)
        def _():
            landed(home + d, k).wait_recv()

            @pl.when(has_below)
            def _():
                go_down(d, k).start()

            go_over(home + d, k).start()

        @pl.when(pair - d > 0)
        def _():
            landed(home - d, k).wait_recv()

            @pl.when(has_above)
            def _():
                go_up(d, k).start()

            go_over(home - d, k).start()

    def last(d):
        @pl.when(pair + d == top)
        def _():
            shared_arrival(0).wait_recv()
            shared_over(0).start()
            shared_crossed(0).wait_recv()

            @pl.when(has_below)
            def _():
                share(to_below, from_above)
                shared_down().start()

            for k in range(1, PIECES):
                landed(home + d, k).wait_recv()

                @pl.when(has_below)
                def _(k=k):
                    go_down(d, k).start()

                go_over(home + d, k).start()

        @pl.when(pair - d == 0)
        def _():
            shared_arrival(1).wait_recv()
            shared_over(1).start()
            shared_crossed(1).wait_recv()

            @pl.when(has_above)
            def _():
                share(to_above, from_below)
                shared_up().start()

            for k in range(1, PIECES):
                landed(home - d, k).wait_recv()

                @pl.when(has_above)
                def _(k=k):
                    go_up(d, k).start()

                go_over(home - d, k).start()

    def middles(d):
        for k in range(1, PIECES):
            middle(d, k)

    forward(1, 0)
    flags_on(1)
    middles(1)
    last(1)
    forward(2, 0)
    h_wait(beside, NEAR, 0)
    relay_across = h_put(beside, 0, FAR, 2, (across, col))
    relay_across.start()
    h_wait(across, OVER, 1)
    relay_beside = h_put(across, 1, FAR, 3, (beside, col))
    relay_beside.start()
    flags_on(2)
    middles(2)
    flags_on(3)

    totals[0] = jnp.where(pair > 0, own_both, 0)
    totals[1] = jnp.where(pair < top, own_both, 0)
    for side, way in ((0, 1), (1, -1)):
        starts[home, side] = jnp.int32(0)
        for d in range(1, panels):
            o, n = home + way * d, pair + way * d

            @pl.when((n >= 0) & (n <= top))
            def _(o=o, n=n, side=side):
                at_same, at_other = tabulate(o, 0), tabulate(o, 1)
                start = starts[home, side]
                starts[o, 0] = start + jnp.where(core == 0, 0, at_other)
                starts[o, 1] = start + jnp.where(core == 0, at_same, 0)
                starts[home, side] = start + at_same + at_other
                totals[0] += jnp.where(n > 0, at_same + at_other, 0)
                totals[1] += jnp.where(n < top, at_same + at_other, 0)

    line_over[0, 0] = jnp.maximum(totals[0] - shared, 0) + jnp.maximum(totals[1] - shared, 0)

    def agree(n, device):
        return put(line_over.at[2 * n], line_over.at[2 * n + 1], over_sent.at[n], over_landed.at[n], device)

    agree(0, (beside, col)).start()
    last(2)

    def fill(o, side):
        source = (from_above, from_below)[side]
        for n in range(rest):
            same[o][base + n] = source[within(starts[o, 0] + n, shared)]
            other[o][base + n] = source[within(starts[o, 1] + n, shared)]

    def spread(o, way_d):
        dense(o, 0, pair + way_d, every_row)
        dense(o, 1, pair + way_d, every_row)

    h_wait(beside, NEAR, 1)
    h_wait(across, OVER, 0)
    @pl.when((pair != row) & (pair != opposite))
    def _():
        add(pair)

    sides = ((0, 1), (1, -1))

    def at_end(body):
        for side, way in sides:
            @pl.when(pair == (0, top)[side])
            def _(side=side, way=way):
                body(side, home + way * far, pair + way * far)

    def far_first(side, o, panel):
        landed(o, 0).wait_recv()
        go_over(o, 0).start()
        shared_arrival(side).wait_recv()
        shared_over(side).start()
        shared_crossed(side).wait_recv()

    at_end(far_first)
    agree(0, (beside, col)).wait_recv()
    line_over[2, 0] = line_over[0, 0] + line_over[1, 0]
    agree(1, (across, col)).start()

    for side, way in sides:
        for d in range(1, far):
            o, n = home + way * d, pair + way * d

            @pl.when((n >= 0) & (n <= top))
            def _(o=o, side=side, way=way, d=d):
                for k in range(PIECES):
                    crossed(o, k).wait_recv()
                fill(o, side)
                spread(o, way * d)

    def near(panel):
        gap = panel - pair
        return (gap < far) & (gap > -far)

    def near_panel(step, carry):
        panel = (pair + step) % panels

        @pl.when(near(panel) & (panel != opposite))
        def _():
            add(panel)

        return carry

    def far_middle(side, o, panel):
        for k in range(1, PIECES - 1):
            landed(o, k).wait_recv()
            go_over(o, k).start()

    at_end(far_middle)
    lax.fori_loop(1, panels, near_panel, 0)

    h_wait(opposite, FAR, 0)
    h_wait(opposite, FAR, 1)

    @pl.when(near(opposite))
    def _():
        add(opposite)

    is_end = (pair == 0) | (pair == top)

    def far_rows(side, o, panel):
        for k in range(PIECES - 1):
            crossed(o, k).wait_recv()
        fill(o, side)
        dense(o, 0, panel, range(1))
        dense(o, 1, panel, range(1))

    at_end(far_rows)

    @pl.when(is_end)
    def _():
        panel = top - pair
        left = w_buf[panel, :, :edge].reshape(2 * edge, width)
        right = h_buf[panel, :, :edge].reshape(2 * edge, h_buf.shape[3])
        total[...] += contract(left, right)

    def far_same(side, o, panel):
        landed(o, PIECES - 1).wait_recv()
        go_over(o, PIECES - 1).start()
        same[o][final_piece] = late_same[side ^ 1][...]
        dense(o, 0, panel, later_rows)

    at_end(far_same)

    @pl.when(is_end)
    def _():
        panel = top - pair
        total[...] += contract(w_buf[panel, core, edge:], h_buf[panel, core, edge:])

    def far_other(side, o, panel):
        crossed(o, PIECES - 1).wait_recv()
        other[o][final_piece] = late_other[side ^ 1][...]
        dense(o, 1, panel, later_rows)

    at_end(far_other)

    @pl.when(is_end)
    def _():
        panel = top - pair
        final = total[...] + contract(w_buf[panel, 1 - core, edge:], h_buf[panel, 1 - core, edge:])
        out_ref[...] = final.astype(out_ref.dtype)

    @pl.when(jnp.logical_not(is_end))
    def _():
        out_ref[...] = total[...].astype(out_ref.dtype)

    agree(1, (across, col)).wait_recv()
    over_ref[0, 0] = line_over[2, 0] + line_over[3, 0]
    for n in range(2):
        agree(n, (beside, col)).wait_send()
    both_halves = h_buf.at[row]
    for number, device in ((0, (beside, col)), (1, (across, col))):
        put(both_halves, both_halves, h_sent.at[number], h_landed.at[0, 0], device).wait_send()
    relay_across.wait_send()
    relay_beside.wait_send()
    flags_cross(core).wait_send()
    go_over(home, WHOLE).wait_send()

    @pl.when(has_above)
    def _():
        shared_over(0).wait_send()
        shared_up().wait_send()

    @pl.when(has_below)
    def _():
        shared_over(1).wait_send()
        shared_down().wait_send()

    for d in range(far):
        @pl.when(has_below & (pair + d <= top))
        def _(d=d):
            flags_go_down(d).wait_send()
            all_pieces(home + d, down_sent.at[d]).wait_send()

        @pl.when(has_above & (pair - d >= 0))
        def _(d=d):
            flags_go_up(d).wait_send()
            all_pieces(home - d, up_sent.at[d]).wait_send()

    for d in range(1, panels):
        @pl.when(pair + d <= top)
        def _(d=d):
            all_pieces(home + d, core_sent.at[mark(home + d)]).wait_send()

        @pl.when(pair - d >= 0)
        def _(d=d):
            all_pieces(home - d, core_sent.at[mark(home - d)]).wait_send()


def base_slots(blocks):
    return 2 * blocks // 3


PIECES = 3


def piece_cuts(base):
    return (0, base // 3, 7 * base // 12, base)


def packed(weights, weight_flags, hamiltonian, ham_flags):
    weights, weight_flags, hamiltonian, ham_flags = (
        pltpu.with_memory_space_constraint(given, pltpu.HBM)
        for given in (weights, weight_flags, hamiltonian, ham_flags.T)
    )
    panels = lax.axis_size("row")
    half_rows, width = weights.shape
    panel_rows, slice_cols = hamiltonian.shape
    edge = half_rows // weight_flags.shape[0]
    blocks = weight_flags.size
    base = base_slots(blocks)
    shared = base
    cuts = piece_cuts(base)
    offsets = 2 * panels - 1
    dma = pltpu.SemaphoreType.DMA
    hbm = pl.BlockSpec(memory_space=pltpu.HBM)

    def slots(count):
        return pltpu.VMEM((count, edge, edge), jnp.bfloat16)

    out, over = pl.pallas_call(
        functools.partial(packed_kernel, panels),
        out_shape=(
            pltpu.VMEM((width, slice_cols), jnp.bfloat16),
            pltpu.SMEM((1, 1), jnp.int32),
        ),
        in_specs=[hbm] * 4,
        out_specs=(pl.BlockSpec(memory_space=pltpu.VMEM), pl.BlockSpec(memory_space=pltpu.SMEM)),
        scratch_shapes=[
            pltpu.SMEM(ham_flags.shape, ham_flags.dtype),
            [pltpu.SMEM((2, *weight_flags.shape), weight_flags.dtype) for _ in range(offsets)],
            pltpu.SMEM((2 * offsets, blocks), jnp.int32),
            pltpu.SMEM((blocks + 1,), jnp.int32),
            pltpu.SMEM((offsets, 2), jnp.int32),
            pltpu.SMEM((2,), jnp.int32),
            pltpu.SMEM((4, 1), jnp.int32),
            slots(blocks),
            pltpu.VMEM(hamiltonian.shape, hamiltonian.dtype),
            [slots(blocks + 1) for _ in range(offsets)],
            [slots(blocks + 1) for _ in range(offsets)],
            [slots(cuts[-1] - cuts[-2]) for _ in range(2)],
            [slots(cuts[-1] - cuts[-2]) for _ in range(2)],
            slots(shared),
            slots(shared),
            slots(shared // 2),
            slots(shared // 2),
            pltpu.VMEM((panels, 2, half_rows, width), jnp.bfloat16),
            pltpu.VMEM((panels, 2, panel_rows // 2, slice_cols), jnp.bfloat16),
            pltpu.VMEM((width, slice_cols), jnp.float32),
            dma((4,)),
            dma((panels,)),
            dma((panels - 1,)),
            dma((panels - 1,)),
            dma((1,)),
            dma((panels - 1, PIECES)),
            dma((panels, PIECES)),
            dma((panels - 1,)),
            dma((panels - 1,)),
            dma((panels,)),
            dma((2, 2)),
            dma((2,)),
            dma((2,)),
            dma((3, 2)),
            dma((4,)),
            dma((2,)),
            dma((2,)),
        ],
        compiler_params=pltpu.CompilerParams(collective_id=1, has_side_effects=True),
    )(weight_flags, ham_flags, weights, hamiltonian)
    return lax.cond(
        over[0, 0] > 0,
        lambda kept, *given: gathered(*given),
        lambda kept, *given: kept,
        out, weights, weight_flags, hamiltonian, ham_flags,
    )


def solution(mesh):
    placed = (P("col", "row"), P("col", "row"), P("row", "col"), P("row", "col"))
    every_panel = mesh.shape["row"] == STEPS and mesh.shape["col"] == 2 * STEPS
    return jax.shard_map(
        packed if every_panel else shards,
        mesh=mesh, in_specs=placed, out_specs=P("row", "col"), check_vma=False,
    )
```

```python
import functools

import jax
import jax.numpy as jnp
from jax import lax
from jax.experimental import pallas as pl
from jax.experimental.pallas import tpu as pltpu
from jax.sharding import PartitionSpec as P

STEPS = 4


def from_behind(block, axis, distance):
    devices = range(lax.axis_size(axis))
    route = [((i - distance) % len(devices), i) for i in devices]
    return lax.ppermute(block, axis, route)


def from_partner(value, axis, bit):
    mask = 2**bit
    pairs = [(source, source ^ mask) for source in range(lax.axis_size(axis))]
    return lax.ppermute(value, axis, pairs)


def masked(dense_tile, flag_grid):
    row_blocks, col_blocks = flag_grid.shape
    block_edge = dense_tile.shape[0] // row_blocks
    shaped = dense_tile.reshape(row_blocks, block_edge, col_blocks, block_edge)
    retain = (flag_grid > 0)[:, None, :, None]
    return jnp.where(retain, shaped, jnp.zeros_like(shaped)).reshape(dense_tile.shape)


def aligned(operand, amount, bit_count, mover):
    for level in range(bit_count):
        moved = mover(operand, level)
        chosen = (amount >> level) % 2 == 1
        operand = jnp.where(chosen, moved, operand)
    return operand


def contract(left_part, right_part):
    return lax.dot_general(
        left_part, right_part, (((0,), (0,)), ((), ())), preferred_element_type=jnp.float32
    )


def shards(weights, weight_flags, hamiltonian, ham_flags):
    row_count = lax.axis_size("row")
    bit_count = (row_count - 1).bit_length()
    row_index = lax.axis_index("row")
    col_index = lax.axis_index("col")
    pair_index = col_index // 2
    parity = col_index % 2
    w_masked = masked(weights, weight_flags)
    h_masked = masked(hamiltonian, ham_flags)
    ham_tile = aligned(
        h_masked,
        pair_index,
        bit_count,
        lambda operand, level: from_behind(operand, "row", -(1 << level)),
    )
    w_half = aligned(
        w_masked,
        row_index,
        bit_count,
        lambda operand, level: from_behind(operand, "col", -(2 << level)),
    )
    half_rows = ham_tile.shape[0] // 2
    upper_rows = ham_tile[:half_rows]
    lower_rows = ham_tile[half_rows:]
    retained = jnp.where(parity == 0, upper_rows, lower_rows)
    handed = jnp.where(parity == 0, lower_rows, upper_rows)
    received = from_partner(handed, "col", 0)
    joined = jnp.where(
        parity == 0,
        jnp.concatenate((retained, received), 1),
        jnp.concatenate((received, retained), 1),
    )
    summed = contract(w_half, joined)
    for step_index in range(1, STEPS):
        w_half = from_behind(w_half, "col", -2)
        joined = from_behind(joined, "row", -1)
        summed = summed + contract(w_half, joined)
    half_width = summed.shape[1] // 2
    own_part = jnp.where(parity == 0, summed[:, :half_width], summed[:, half_width:])
    their_part = jnp.where(parity == 0, summed[:, half_width:], summed[:, :half_width])
    summed = own_part + from_partner(their_part, "col", 0)
    return summed.astype(jnp.bfloat16)


SHARES = (5, 3)
CHUNKS = len(SHARES)
MESH = pl.DeviceIdType.MESH


def put(source, target, sent, landed, device):
    return pltpu.make_async_remote_copy(
        src_ref=source,
        dst_ref=target,
        send_sem=sent,
        recv_sem=landed,
        device_id=device,
        device_id_type=MESH,
    )


def gather_kernel(
    panels, w_flags_hbm, h_flags_hbm, w_hbm, h_hbm, out_ref, w_flags, h_flags, w_ref, h_ref, w_buf, h_buf, total,
    loaded, w_landed, up_sent, down_sent, core_sent, h_landed, h_sent,
):
    row = lax.axis_index("row")
    col = lax.axis_index("col")
    pair = col // 2
    core = col % 2
    partner = (row, pair * 2 + 1 - core)
    above = (row, col + 2)
    below = (row, col - 2)
    beside = row + 1 - 2 * (row % 2)
    across = (row + panels // 2) % panels
    opposite = (beside + panels // 2) % panels
    has_above = pair < panels - 1
    has_below = pair > 0

    loads = [
        pltpu.make_async_copy(source, target, loaded.at[n])
        for n, (source, target) in enumerate(
            ((w_flags_hbm, w_flags), (w_hbm, w_ref), (h_flags_hbm, h_flags), (h_hbm, h_ref))
        )
    ]
    for load in loads:
        load.start()

    barrier = pltpu.get_barrier_semaphore()

    def greet(device):
        pl.semaphore_signal(barrier, inc=1, device_id=device, device_id_type=MESH)

    greet(partner)
    greet((beside, col))
    greet((across, col))

    @pl.when(has_above)
    def _():
        greet(above)

    @pl.when(has_below)
    def _():
        greet(below)

    loads[0].wait()
    loads[1].wait()
    half_rows, width = w_ref.shape
    edge = half_rows // w_flags.shape[0]
    bounds = [half_rows * sum(SHARES[:k]) // sum(SHARES) for k in range(CHUNKS + 1)]
    for r in range(w_flags.shape[0]):
        for c in range(w_flags.shape[1]):
            rows, lanes = slice(r * edge, (r + 1) * edge), slice(c * edge, (c + 1) * edge)
            block = w_ref[rows, lanes]
            kept = jnp.where(w_flags[r, c] > 0, block, jnp.zeros_like(block))
            w_buf[pair, core, rows, lanes] = kept
    pl.semaphore_wait(
        barrier, 3 + has_above.astype(jnp.int32) + has_below.astype(jnp.int32)
    )

    def piece(k):
        return slice(bounds[k], bounds[k + 1])

    def go_up(panel, k):
        slot = w_buf.at[panel, core, piece(k)]
        return put(slot, slot, up_sent.at[panel, k], w_landed.at[panel, core, k], above)

    def go_down(panel, k):
        slot = w_buf.at[panel, core, piece(k)]
        return put(slot, slot, down_sent.at[panel, k], w_landed.at[panel, core, k], below)

    def go_over(panel, k):
        slot = w_buf.at[panel, core, piece(k)]
        return put(slot, slot, core_sent.at[panel, k], w_landed.at[panel, core, k], partner)

    def arrival(panel, half, k):
        slot = w_buf.at[panel, half, piece(k)]
        return put(slot, slot, core_sent.at[panel, k], w_landed.at[panel, half, k], partner)

    def h_put(panel, half, number, device):
        slot = h_buf.at[panel, half]
        return put(slot, slot, h_sent.at[number], h_landed.at[panel, half], device)

    def each(body):
        for k in range(CHUNKS):
            body(k)

    def first_sends(k):
        @pl.when(has_above)
        def _():
            go_up(pair, k).start()

        @pl.when(has_below)
        def _():
            go_down(pair, k).start()

    each(first_sends)
    loads[2].wait()
    loads[3].wait()
    for r in range(h_flags.shape[1]):
        for c in range(h_flags.shape[0]):
            lanes = slice(c * edge, (c + 1) * edge)
            block = h_ref[r * edge:(r + 1) * edge, lanes]
            half, start = divmod(r * edge, half_rows)
            kept = jnp.where(h_flags[c, r] > 0, block, jnp.zeros_like(block))
            h_buf[row, half, start:start + edge, lanes] = kept

    h_copies = [
        h_put(row, 0, 0, (beside, col)),
        h_put(row, 1, 1, (across, col)),
        h_put(row, 1, 2, (beside, col)),
        h_put(row, 0, 3, (across, col)),
    ]
    for copy in h_copies:
        copy.start()
    each(lambda k: go_over(pair, k).start())

    def relay(distance, k):
        @pl.when(pair >= distance)
        def _():
            panel = pair - distance
            arrival(panel, core, k).wait_recv()

            @pl.when(has_above)
            def _():
                go_up(panel, k).start()

            go_over(panel, k).start()

        @pl.when(pair + distance < panels)
        def _():
            panel = pair + distance
            arrival(panel, core, k).wait_recv()

            @pl.when(has_below)
            def _():
                go_down(panel, k).start()

            go_over(panel, k).start()

    each(functools.partial(relay, 1))
    h_put(beside, 0, 0, (beside, col)).wait_recv()
    relay_across = h_put(beside, 0, 4, (across, col))
    relay_across.start()
    h_put(across, 1, 0, (beside, col)).wait_recv()
    relay_beside = h_put(across, 1, 5, (beside, col))
    relay_beside.start()
    for distance in range(2, panels - 1):
        each(functools.partial(relay, distance))
    h_put(beside, 1, 0, (beside, col)).wait_recv()
    h_put(across, 0, 0, (beside, col)).wait_recv()
    h_put(opposite, 0, 0, (beside, col)).wait_recv()
    h_put(opposite, 1, 0, (beside, col)).wait_recv()

    total[...] = jnp.zeros_like(total)
    span = 2 * half_rows

    def near_panel(step, carry):
        panel = (pair + step) % panels
        gap = panel - pair

        @pl.when((gap < panels - 1) & (gap > 1 - panels))
        def _():
            each(lambda k: arrival(panel, 1 - core, k).wait_recv())
            left = w_buf[panel].reshape(span, width)
            right = h_buf[panel].reshape(span, h_buf.shape[3])
            total[...] += contract(left, right)

        return carry

    lax.fori_loop(0, panels, near_panel, 0)

    is_end = (pair == 0) | (pair == panels - 1)

    @pl.when(is_end)
    def _():
        panel = panels - 1 - pair

        def product(half, k):
            return contract(w_buf[panel, half, piece(k)], h_buf[panel, half, piece(k)])

        for k in range(CHUNKS - 1):
            arrival(panel, core, k).wait_recv()
            go_over(panel, k).start()
            total[...] += product(core, k)
            arrival(panel, 1 - core, k).wait_recv()
            total[...] += product(1 - core, k)

        last = CHUNKS - 1
        arrival(panel, core, last).wait_recv()
        go_over(panel, last).start()
        total[...] += product(core, last)
        arrival(panel, 1 - core, last).wait_recv()
        out_ref[...] = (total[...] + product(1 - core, last)).astype(out_ref.dtype)

    @pl.when(jnp.logical_not(is_end))
    def _():
        out_ref[...] = total[...].astype(out_ref.dtype)

    for copy in h_copies + [relay_across, relay_beside]:
        copy.wait_send()

    def drain(panel, carry):
        def one(k):
            go_over(panel, k).wait_send()

            @pl.when(has_above & (panel <= pair))
            def _():
                go_up(panel, k).wait_send()

            @pl.when(has_below & (panel >= pair))
            def _():
                go_down(panel, k).wait_send()

        each(one)
        return carry

    lax.fori_loop(0, panels, drain, 0)


def gathered(weights, weight_flags, hamiltonian, ham_flags):
    panels = lax.axis_size("row")
    half_rows, width = weights.shape
    panel_rows, slice_cols = hamiltonian.shape
    dma = pltpu.SemaphoreType.DMA
    vmem = pl.BlockSpec(memory_space=pltpu.VMEM)
    hbm = pl.BlockSpec(memory_space=pltpu.HBM)
    return pl.pallas_call(
        functools.partial(gather_kernel, panels),
        out_shape=pltpu.VMEM((width, slice_cols), jnp.bfloat16),
        in_specs=[hbm] * 4,
        out_specs=vmem,
        scratch_shapes=[
            pltpu.SMEM(weight_flags.shape, weight_flags.dtype),
            pltpu.SMEM(ham_flags.shape, ham_flags.dtype),
            pltpu.VMEM(weights.shape, weights.dtype),
            pltpu.VMEM(hamiltonian.shape, hamiltonian.dtype),
            pltpu.VMEM((panels, 2, half_rows, width), jnp.bfloat16),
            pltpu.VMEM((panels, 2, panel_rows // 2, slice_cols), jnp.bfloat16),
            pltpu.VMEM((width, slice_cols), jnp.float32),
            dma((4,)),
            dma((panels, 2, CHUNKS)),
            dma((panels, CHUNKS)),
            dma((panels, CHUNKS)),
            dma((panels, CHUNKS)),
            dma((panels, 2)),
            dma((6,)),
        ],
        compiler_params=pltpu.CompilerParams(collective_id=0, has_side_effects=True),
    )(weight_flags, ham_flags, weights, hamiltonian)


def packed_kernel(
    panels, w_flags_hbm, h_flags_hbm, w_hbm, h_hbm, out_ref, over_ref,
    h_flags, flags, places, first_from, starts, totals, line_over,
    w_blocks, h_ref, same, other, late_same, late_other, from_above, from_below, to_below, to_above, w_buf, h_buf, total,
    loaded, flags_landed, flags_down, flags_up, flags_core, same_landed, other_landed, down_sent, up_sent, core_sent,
    shared_landed, shared_sent, shared_core_sent, h_landed, h_sent, over_landed, over_sent,
):
    row = lax.axis_index("row")
    col = lax.axis_index("col")
    pair = col // 2
    core = col % 2
    partner = (row, pair * 2 + 1 - core)
    above = (row, col + 2)
    below = (row, col - 2)
    beside = row + 1 - 2 * (row % 2)
    across = (row + panels // 2) % panels
    opposite = (beside + panels // 2) % panels
    top = panels - 1
    has_above = pair < top
    has_below = pair > 0
    home = top
    w_flags = flags[home].at[core]
    row_blocks, col_blocks = w_flags.shape
    blocks, edge = w_blocks.shape[0], w_blocks.shape[1]
    half_rows = row_blocks * edge
    shared = from_above.shape[0]
    part = shared // 2
    base = base_slots(blocks)
    rest = blocks - base
    cuts = piece_cuts(base)
    slices = [slice(*cuts[k:k + 2]) for k in range(PIECES)]
    final_piece = slices[-1]
    WHOLE = 0
    far = top
    edges = (home - far, home + far)

    flag_load = pltpu.make_async_copy(w_flags_hbm, w_flags, loaded.at[0])
    flag_load.start()
    for b in range(blocks):
        r, c = divmod(b, col_blocks)
        source = w_hbm.at[r * edge:(r + 1) * edge, c * edge:(c + 1) * edge]
        pltpu.make_async_copy(source, w_blocks.at[b], loaded.at[3]).start()
    h_loads = [
        pltpu.make_async_copy(h_flags_hbm, h_flags, loaded.at[1]),
        pltpu.make_async_copy(h_hbm, h_ref, loaded.at[2]),
    ]
    for load in h_loads:
        load.start()

    barrier = pltpu.get_barrier_semaphore()

    def greet(device):
        pl.semaphore_signal(barrier, inc=1, device_id=device, device_id_type=MESH)

    greet(partner)
    greet((beside, col))
    greet((across, col))

    @pl.when(has_above)
    def _():
        greet(above)

    @pl.when(has_below)
    def _():
        greet(below)

    def piece(refs, late, o, k):
        if o in edges and k == PIECES - 1:
            return late[edges.index(o)]
        return refs[o].at[slices[k]]

    def mark(o):
        return (o - home) % panels - 1

    def go_down(d, k):
        source, target = (piece(same, late_same, home + n, k) for n in (d, d + 1))
        return put(source, target, down_sent.at[d], same_landed.at[mark(home + d + 1), k], below)

    def go_up(d, k):
        source, target = (piece(same, late_same, home - n, k) for n in (d, d + 1))
        return put(source, target, up_sent.at[d], same_landed.at[mark(home - d - 1), k], above)

    def go_over(o, k):
        if o == home:
            return put(same[o].at[:blocks], other[o].at[:blocks], core_sent.at[top], other_landed.at[top, 0], partner)
        source, target = piece(same, late_same, o, k), piece(other, late_other, o, k)
        return put(source, target, core_sent.at[mark(o)], other_landed.at[mark(o), k], partner)

    def flags_go_down(d):
        source, target = flags[home + d], flags[home + d + 1]
        return put(source, target, flags_down.at[d], flags_landed.at[mark(home + d + 1)], below)

    def flags_go_up(d):
        source, target = flags[home - d], flags[home - d - 1]
        return put(source, target, flags_up.at[d], flags_landed.at[mark(home - d - 1)], above)

    def flags_arrival(o):
        return put(flags[o], flags[o], flags_core.at[0], flags_landed.at[mark(o)], partner)

    def flags_cross(half):
        slot = flags[home].at[half]
        return put(slot, slot, flags_core.at[0], flags_landed.at[top], partner)

    def landed(o, k):
        slot = piece(same, late_same, o, k)
        return put(slot, slot, core_sent.at[0], same_landed.at[mark(o), k], partner)

    def crossed(o, k):
        return go_over(o, k)

    def all_pieces(o, sent):
        slot = same[o].at[:base]
        return put(slot, slot, sent, same_landed.at[0, 0], partner)

    def shared_half(ref, half):
        return ref.at[pl.ds(half * part, part)]

    def shared_down():
        return put(to_below, shared_half(from_above, core), shared_sent.at[0], shared_landed.at[0, 0], below)

    def shared_up():
        return put(to_above, shared_half(from_below, core), shared_sent.at[1], shared_landed.at[1, 0], above)

    def shared_over(side):
        slot = shared_half((from_above, from_below)[side], core)
        return put(slot, slot, shared_core_sent.at[side], shared_landed.at[side, 1], partner)

    def shared_arrival(side):
        slot = shared_half((from_above, from_below)[side], core)
        return put(slot, slot, shared_core_sent.at[side], shared_landed.at[side, 0], partner)

    def shared_crossed(side):
        slot = shared_half((from_above, from_below)[side], 1 - core)
        return put(slot, slot, shared_core_sent.at[side], shared_landed.at[side, 1], partner)

    NEAR, OVER, FAR = 0, 1, 2

    def h_put(panel, half, mark, sent, device):
        slot = h_buf.at[panel, half]
        return put(slot, slot, h_sent.at[sent], h_landed.at[mark, half], device)

    def h_wait(panel, mark, half):
        h_put(panel, half, mark, 0, (beside, col)).wait_recv()

    flag_load.wait()
    nearest = jnp.int32(blocks - 1)
    first_from[blocks] = nearest
    for b in reversed(range(blocks)):
        nearest = jnp.where(flags[home][core, b // col_blocks, b % col_blocks] > 0, b, nearest)
        first_from[b] = nearest
    pltpu.make_async_copy(same[home].at[:blocks], w_blocks, loaded.at[3]).wait()

    def pack(start, stop, chosen):
        for k in range(start, stop):
            same[home][k] = w_blocks[chosen]
            chosen = first_from[chosen + 1]
        return chosen

    chosen = pack(0, slices[0].stop, first_from[0])
    pl.semaphore_wait(
        barrier, 3 + has_above.astype(jnp.int32) + has_below.astype(jnp.int32)
    )

    def both_ways(k, down, up):
        @pl.when(down)
        def _():
            go_down(0, k).start()

        @pl.when(up)
        def _():
            go_up(0, k).start()

    both_ways(0, has_below, has_above)
    flags_cross(core).start()
    pack(slices[1].start, blocks, chosen)
    go_over(home, WHOLE).start()
    for load in h_loads:
        load.wait()
    for r in range(h_flags.shape[1]):
        for c in range(h_flags.shape[0]):
            lanes = slice(c * edge, (c + 1) * edge)
            block = h_ref[r * edge:(r + 1) * edge, lanes]
            half, start = divmod(r * edge, half_rows)
            kept = jnp.where(h_flags[c, r] > 0, block, jnp.zeros_like(block))
            h_buf[row, half, start:start + edge, lanes] = kept

    h_put(row, 0, NEAR, 0, (beside, col)).start()
    h_put(row, 1, OVER, 1, (across, col)).start()
    h_put(row, 1, NEAR, 0, (beside, col)).start()
    h_put(row, 0, OVER, 1, (across, col)).start()

    flags_cross(1 - core).wait_recv()

    @pl.when(has_below)
    def _():
        flags_go_down(0).start()

    @pl.when(has_above)
    def _():
        flags_go_up(0).start()

    for k in range(1, PIECES):
        both_ways(k, has_below & (pair < top), has_above & (pair > 0))

    def tabulate(o, which):
        half = core if which == 0 else 1 - core
        position = jnp.int32(0)
        for b in range(blocks):
            present = flags[o][half, b // col_blocks, b % col_blocks] > 0
            places[2 * o + which, b] = jnp.where(present, position, blocks)
            position = position + present.astype(jnp.int32)
        return jnp.maximum(position - base, 0)

    own_same = tabulate(home, 0)
    own_other = tabulate(home, 1)
    own_both = own_same + own_other
    same_start = jnp.where(core == 0, 0, own_other)
    other_start = jnp.where(core == 0, own_same, 0)

    def within(index, limit):
        return jnp.minimum(jnp.maximum(index, 0), limit - 1)

    def share(target, source):
        for n in range(part):
            slot = core * part + n
            in_same, in_other = slot - same_start, slot - other_start
            value = other[home][base + within(in_other, rest)]
            if source is not None:
                passed = source[within(slot - own_both, shared)]
                value = jnp.where((in_other >= 0) & (in_other < own_other), value, passed)
            mine = same[home][base + within(in_same, rest)]
            target[n] = jnp.where((in_same >= 0) & (in_same < own_same), mine, value)

    crossed(home, WHOLE).wait_recv()

    @pl.when(pair == top)
    def _():
        share(to_below, None)
        shared_down().start()
        for k in range(1, PIECES):
            go_down(0, k).start()

    @pl.when(pair == 0)
    def _():
        share(to_above, None)
        shared_up().start()
        for k in range(1, PIECES):
            go_up(0, k).start()

    def dense(o, which, panel, wanted):
        packed = (same, other)[which][o]
        half = core if which == 0 else 1 - core
        for r in wanted:
            for c in range(col_blocks):
                rows, lanes = slice(r * edge, (r + 1) * edge), slice(c * edge, (c + 1) * edge)
                w_buf[panel, half, rows, lanes] = packed[places[2 * o + which, r * col_blocks + c]]

    every_row = range(row_blocks)
    later_rows = range(1, row_blocks)
    for packed in (*same, *other):
        packed[blocks] = jnp.zeros((edge, edge), packed.dtype)
    dense(home, 0, pair, every_row)
    dense(home, 1, pair, every_row)
    total[...] = jnp.zeros_like(total)
    span = 2 * half_rows
    width = col_blocks * edge

    def add(panel):
        left = w_buf[panel].reshape(span, width)
        right = h_buf[panel].reshape(span, h_buf.shape[3])
        total[...] += contract(left, right)

    @pl.when(pair == row)
    def _():
        add(pair)

    def forward(d, k):
        @pl.when(pair + d <= top)
        def _():
            landed(home + d, k).wait_recv()

            @pl.when(has_below)
            def _():
                go_down(d, k).start()

            go_over(home + d, k).start()

        @pl.when(pair - d >= 0)
        def _():
            landed(home - d, k).wait_recv()

            @pl.when(has_above)
            def _():
                go_up(d, k).start()

            go_over(home - d, k).start()

    def flags_on(d):
        @pl.when(pair + d <= top)
        def _():
            flags_arrival(home + d).wait_recv()

            if d < top:
                @pl.when(has_below)
                def _():
                    flags_go_down(d).start()

        @pl.when(pair - d >= 0)
        def _():
            flags_arrival(home - d).wait_recv()

            if d < top:
                @pl.when(has_above)
                def _():
                    flags_go_up(d).start()

    def middle(d, k):
        @pl.when(pair + d < top)
        def _():
            landed(home + d, k).wait_recv()

            @pl.when(has_below)
            def _():
                go_down(d, k).start()

            go_over(home + d, k).start()

        @pl.when(pair - d > 0)
        def _():
            landed(home - d, k).wait_recv()

            @pl.when(has_above)
            def _():
                go_up(d, k).start()

            go_over(home - d, k).start()

    def last(d):
        @pl.when(pair + d == top)
        def _():
            shared_arrival(0).wait_recv()
            shared_over(0).start()
            shared_crossed(0).wait_recv()

            @pl.when(has_below)
            def _():
                share(to_below, from_above)
                shared_down().start()

            for k in range(1, PIECES):
                landed(home + d, k).wait_recv()

                @pl.when(has_below)
                def _(k=k):
                    go_down(d, k).start()

                go_over(home + d, k).start()

        @pl.when(pair - d == 0)
        def _():
            shared_arrival(1).wait_recv()
            shared_over(1).start()
            shared_crossed(1).wait_recv()

            @pl.when(has_above)
            def _():
                share(to_above, from_below)
                shared_up().start()

            for k in range(1, PIECES):
                landed(home - d, k).wait_recv()

                @pl.when(has_above)
                def _(k=k):
                    go_up(d, k).start()

                go_over(home - d, k).start()

    def middles(d):
        for k in range(1, PIECES):
            middle(d, k)

    forward(1, 0)
    flags_on(1)
    middles(1)
    last(1)
    forward(2, 0)
    h_wait(beside, NEAR, 0)
    relay_across = h_put(beside, 0, FAR, 2, (across, col))
    relay_across.start()
    h_wait(across, OVER, 1)
    relay_beside = h_put(across, 1, FAR, 3, (beside, col))
    relay_beside.start()
    flags_on(2)
    middles(2)
    flags_on(3)

    totals[0] = jnp.where(pair > 0, own_both, 0)
    totals[1] = jnp.where(pair < top, own_both, 0)
    for side, way in ((0, 1), (1, -1)):
        starts[home, side] = jnp.int32(0)
        for d in range(1, panels):
            o, n = home + way * d, pair + way * d

            @pl.when((n >= 0) & (n <= top))
            def _(o=o, n=n, side=side):
                at_same, at_other = tabulate(o, 0), tabulate(o, 1)
                start = starts[home, side]
                starts[o, 0] = start + jnp.where(core == 0, 0, at_other)
                starts[o, 1] = start + jnp.where(core == 0, at_same, 0)
                starts[home, side] = start + at_same + at_other
                totals[0] += jnp.where(n > 0, at_same + at_other, 0)
                totals[1] += jnp.where(n < top, at_same + at_other, 0)

    line_over[0, 0] = jnp.maximum(totals[0] - shared, 0) + jnp.maximum(totals[1] - shared, 0)

    def agree(n, device):
        return put(line_over.at[2 * n], line_over.at[2 * n + 1], over_sent.at[n], over_landed.at[n], device)

    agree(0, (beside, col)).start()
    last(2)

    def fill(o, side):
        source = (from_above, from_below)[side]
        for n in range(rest):
            same[o][base + n] = source[within(starts[o, 0] + n, shared)]
            other[o][base + n] = source[within(starts[o, 1] + n, shared)]

    def spread(o, way_d):
        dense(o, 0, pair + way_d, every_row)
        dense(o, 1, pair + way_d, every_row)

    h_wait(beside, NEAR, 1)
    h_wait(across, OVER, 0)
    @pl.when((pair != row) & (pair != opposite))
    def _():
        add(pair)

    sides = ((0, 1), (1, -1))

    def at_end(body):
        for side, way in sides:
            @pl.when(pair == (0, top)[side])
            def _(side=side, way=way):
                body(side, home + way * far, pair + way * far)

    def far_first(side, o, panel):
        landed(o, 0).wait_recv()
        go_over(o, 0).start()
        shared_arrival(side).wait_recv()
        shared_over(side).start()
        shared_crossed(side).wait_recv()

    at_end(far_first)
    agree(0, (beside, col)).wait_recv()
    line_over[2, 0] = line_over[0, 0] + line_over[1, 0]
    agree(1, (across, col)).start()

    for side, way in sides:
        for d in range(1, far):
            o, n = home + way * d, pair + way * d

            @pl.when((n >= 0) & (n <= top))
            def _(o=o, side=side, way=way, d=d):
                for k in range(PIECES):
                    crossed(o, k).wait_recv()
                fill(o, side)
                spread(o, way * d)

    def near(panel):
        gap = panel - pair
        return (gap < far) & (gap > -far)

    def near_panel(step, carry):
        panel = (pair + jnp.where(pair == top, panels - step, step)) % panels

        @pl.when(near(panel) & (panel != opposite))
        def _():
            add(panel)

        return carry

    def far_middle(side, o, panel):
        for k in range(1, PIECES - 1):
            landed(o, k).wait_recv()
            go_over(o, k).start()

    lax.fori_loop(1, 2, near_panel, 0)
    at_end(far_middle)
    lax.fori_loop(2, panels, near_panel, 0)

    h_wait(opposite, FAR, 0)
    h_wait(opposite, FAR, 1)

    @pl.when(near(opposite))
    def _():
        add(opposite)

    is_end = (pair == 0) | (pair == top)

    def far_rows(side, o, panel):
        for k in range(PIECES - 1):
            crossed(o, k).wait_recv()
        fill(o, side)
        dense(o, 0, panel, range(1))
        dense(o, 1, panel, range(1))

    at_end(far_rows)

    @pl.when(is_end)
    def _():
        panel = top - pair
        left = w_buf[panel, :, :edge].reshape(2 * edge, width)
        right = h_buf[panel, :, :edge].reshape(2 * edge, h_buf.shape[3])
        total[...] += contract(left, right)

    def far_same(side, o, panel):
        landed(o, PIECES - 1).wait_recv()
        go_over(o, PIECES - 1).start()
        same[o][final_piece] = late_same[side ^ 1][...]
        dense(o, 0, panel, later_rows)

    at_end(far_same)

    @pl.when(is_end)
    def _():
        panel = top - pair
        total[...] += contract(w_buf[panel, core, edge:], h_buf[panel, core, edge:])

    def far_other(side, o, panel):
        crossed(o, PIECES - 1).wait_recv()
        other[o][final_piece] = late_other[side ^ 1][...]
        dense(o, 1, panel, later_rows)

    at_end(far_other)

    @pl.when(is_end)
    def _():
        panel = top - pair
        final = total[...] + contract(w_buf[panel, 1 - core, edge:], h_buf[panel, 1 - core, edge:])
        out_ref[...] = final.astype(out_ref.dtype)

    @pl.when(jnp.logical_not(is_end))
    def _():
        out_ref[...] = total[...].astype(out_ref.dtype)

    agree(1, (across, col)).wait_recv()
    over_ref[0, 0] = line_over[2, 0] + line_over[3, 0]
    for n in range(2):
        agree(n, (beside, col)).wait_send()
    both_halves = h_buf.at[row]
    for number, device in ((0, (beside, col)), (1, (across, col))):
        put(both_halves, both_halves, h_sent.at[number], h_landed.at[0, 0], device).wait_send()
    relay_across.wait_send()
    relay_beside.wait_send()
    flags_cross(core).wait_send()
    go_over(home, WHOLE).wait_send()

    @pl.when(has_above)
    def _():
        shared_over(0).wait_send()
        shared_up().wait_send()

    @pl.when(has_below)
    def _():
        shared_over(1).wait_send()
        shared_down().wait_send()

    for d in range(far):
        @pl.when(has_below & (pair + d <= top))
        def _(d=d):
            flags_go_down(d).wait_send()
            all_pieces(home + d, down_sent.at[d]).wait_send()

        @pl.when(has_above & (pair - d >= 0))
        def _(d=d):
            flags_go_up(d).wait_send()
            all_pieces(home - d, up_sent.at[d]).wait_send()

    for d in range(1, panels):
        @pl.when(pair + d <= top)
        def _(d=d):
            all_pieces(home + d, core_sent.at[mark(home + d)]).wait_send()

        @pl.when(pair - d >= 0)
        def _(d=d):
            all_pieces(home - d, core_sent.at[mark(home - d)]).wait_send()


def base_slots(blocks):
    return 2 * blocks // 3


PIECES = 3


def piece_cuts(base):
    return (0, base // 3, 7 * base // 12, base)


def packed(weights, weight_flags, hamiltonian, ham_flags):
    weights, weight_flags, hamiltonian, ham_flags = (
        pltpu.with_memory_space_constraint(given, pltpu.HBM)
        for given in (weights, weight_flags, hamiltonian, ham_flags.T)
    )
    panels = lax.axis_size("row")
    half_rows, width = weights.shape
    panel_rows, slice_cols = hamiltonian.shape
    edge = half_rows // weight_flags.shape[0]
    blocks = weight_flags.size
    base = base_slots(blocks)
    shared = base
    cuts = piece_cuts(base)
    offsets = 2 * panels - 1
    dma = pltpu.SemaphoreType.DMA
    hbm = pl.BlockSpec(memory_space=pltpu.HBM)

    def slots(count):
        return pltpu.VMEM((count, edge, edge), jnp.bfloat16)

    out, over = pl.pallas_call(
        functools.partial(packed_kernel, panels),
        out_shape=(
            pltpu.VMEM((width, slice_cols), jnp.bfloat16),
            pltpu.SMEM((1, 1), jnp.int32),
        ),
        in_specs=[hbm] * 4,
        out_specs=(pl.BlockSpec(memory_space=pltpu.VMEM), pl.BlockSpec(memory_space=pltpu.SMEM)),
        scratch_shapes=[
            pltpu.SMEM(ham_flags.shape, ham_flags.dtype),
            [pltpu.SMEM((2, *weight_flags.shape), weight_flags.dtype) for _ in range(offsets)],
            pltpu.SMEM((2 * offsets, blocks), jnp.int32),
            pltpu.SMEM((blocks + 1,), jnp.int32),
            pltpu.SMEM((offsets, 2), jnp.int32),
            pltpu.SMEM((2,), jnp.int32),
            pltpu.SMEM((4, 1), jnp.int32),
            slots(blocks),
            pltpu.VMEM(hamiltonian.shape, hamiltonian.dtype),
            [slots(blocks + 1) for _ in range(offsets)],
            [slots(blocks + 1) for _ in range(offsets)],
            [slots(cuts[-1] - cuts[-2]) for _ in range(2)],
            [slots(cuts[-1] - cuts[-2]) for _ in range(2)],
            slots(shared),
            slots(shared),
            slots(shared // 2),
            slots(shared // 2),
            pltpu.VMEM((panels, 2, half_rows, width), jnp.bfloat16),
            pltpu.VMEM((panels, 2, panel_rows // 2, slice_cols), jnp.bfloat16),
            pltpu.VMEM((width, slice_cols), jnp.float32),
            dma((4,)),
            dma((panels,)),
            dma((panels - 1,)),
            dma((panels - 1,)),
            dma((1,)),
            dma((panels - 1, PIECES)),
            dma((panels, PIECES)),
            dma((panels - 1,)),
            dma((panels - 1,)),
            dma((panels,)),
            dma((2, 2)),
            dma((2,)),
            dma((2,)),
            dma((3, 2)),
            dma((4,)),
            dma((2,)),
            dma((2,)),
        ],
        compiler_params=pltpu.CompilerParams(collective_id=1, has_side_effects=True),
    )(weight_flags, ham_flags, weights, hamiltonian)
    return lax.cond(
        over[0, 0] > 0,
        lambda kept, *given: gathered(*given),
        lambda kept, *given: kept,
        out, weights, weight_flags, hamiltonian, ham_flags,
    )


def solution(mesh):
    placed = (P("col", "row"), P("col", "row"), P("row", "col"), P("row", "col"))
    every_panel = mesh.shape["row"] == STEPS and mesh.shape["col"] == 2 * STEPS
    return jax.shard_map(
        packed if every_panel else shards,
        mesh=mesh, in_specs=placed, out_specs=P("row", "col"), check_vma=False,
    )
```
